256 devices in a mesh: band: 8 (over z), grid: 32 (over y, x, core).
Axes of the slice: x: 4, y: 4, z: 8, core: 2. Of those that a mesh axis runs over, the one named last changes fastest.
Arguments:
- orbitals: bfloat16 [64, 128, 128, 128], P('band', 'grid'), may hold values from -2.09375 to 2.09375
- partners: int32 [32, 6], replicated, may hold values from 0 to 63, as said below
- counts: int32 [32], replicated, may hold values from 1 to 6, 96 in all
Outputs:
- exchange_potential: float32 [32, 128, 128, 128], P('band', 'grid')
The draws below stay inside these ranges and needn't reach their ends.
Inputs may be any that keep to these rules, and one draw needn't show every extreme that they name: `partners`: row t lists 6 different bands, none equal to its own band (t // 4) * 8 + t % 4. The counts sum to exactly 96.
All inputs are finite; a program needn't handle non-finite values.
Results may differ from the reference program's by a relative error of at most 0.0003.
Values may be sent and summed in bfloat16 or wider, within the bound.
A program may use at most 64 MiB of HBM per device.

```python
import math
import jax
import jax.numpy as jnp
import numpy as np
from jax import lax

NZ = 128
NY = 128
NX = 128
OWN = 8
TGT = 4
PART = 6
BANDS = 64
TARGETS = 32


def draw_partners(key, part):
    rows = jnp.arange(TARGETS, dtype=jnp.int32)
    own_band = rows // TGT * OWN + rows % TGT
    row_keys = jax.random.split(key, TARGETS)

    def pick(row_key, band):
        order = jax.random.permutation(row_key, BANDS - 1)[:PART].astype(jnp.int32)
        return order + (order >= band).astype(jnp.int32)
    return jax.vmap(pick)(row_keys, own_band)


def steps_of(key, shape, shards, smallest, top_value):
    factor_of = 1.0
    for axis_at, parts in shards:
        steps = jax.random.uniform(jax.random.fold_in(jax.random.fold_in(key, 6), axis_at), (parts,), jnp.float32, smallest / len(shards), top_value / len(shards))
        factor_of = factor_of * jnp.repeat(jnp.exp(steps), shape[axis_at] // parts).reshape((-1,) + (1,) * (len(shape) - 1 - axis_at))
    return factor_of


def length_profile(amount, total, most, skew):
    loads = [(1 << 20) // math.isqrt(standing ** skew) + 1 for standing in range(2, amount + 1)]
    rest, holding = total - most - (amount - 1), [1] * (amount - 1)
    while rest > 0:
        movable = [i for i in range(amount - 1) if holding[i] < most]
        mass, remaining = sum([loads[i] for i in movable]), rest
        for i in movable:
            extra = min(most - holding[i], max(1, remaining * loads[i] // mass), rest)
            holding[i] = holding[i] + extra
            rest = rest - extra
    return np.array([most] + holding)


def uneven_parts(key, number_of, total, most, slope):
    if number_of == 2:
        one = jax.random.randint(key, (), max(1, total - most), min(most, total - 1) + 1)
        return jnp.stack([one, total - one])
    tallies = jnp.asarray(length_profile(number_of, total, most, slope), jnp.int32)
    pairs = (number_of - 1) // 2
    giver, taker = tallies[1:1 + 2 * pairs:2], tallies[2:2 + 2 * pairs:2]
    room = jnp.minimum(giver - 1, most - taker)
    shifted = jax.random.randint(jax.random.fold_in(key, 1), (pairs,), 0, 1 << 20) % (room + 1)
    tallies = tallies.at[1:1 + 2 * pairs:2].set(giver - shifted).at[2:2 + 2 * pairs:2].set(taker + shifted)
    return tallies[jax.random.permutation(jax.random.fold_in(key, 2), number_of)]


def normal_values(key, extent, scale, bound, pieces=(), held_as=jnp.bfloat16):
    result = jax.random.normal(key, extent, jnp.float32) * scale
    if len(pieces) > 0:
        result = steps_of(key, extent, pieces, -0.22, 0.18) * result
    return jnp.clip(result, min=-bound, max=bound).astype(held_as)


def setup_inputs(seed: int = 0) -> dict:
    key_list = jax.random.split(jax.random.key(seed), 4)
    orbitals = normal_values(key_list[0], (BANDS, NZ, NY, NX), 0.35, 2.09375, ((0, 8), (1, 32)))
    partners = draw_partners(jax.random.fold_in(key_list[3], 71), 0)
    counts = uneven_parts(key_list[2], TARGETS, TARGETS * PART // 2, PART, 2).astype(jnp.int32)
    return dict(orbitals=orbitals, partners=partners, counts=counts)


screening = 0.032


def frequency(length, start, count):
    index = start + jnp.arange(count, dtype=jnp.int32)
    folded = jnp.minimum(index, length - index).astype(jnp.float32)
    return (2.0 * math.pi / length) * folded


def screened_kernel(z_freq, y_freq, x_freq):
    squared = z_freq[:, None, None] ** 2 + y_freq[None, :, None] ** 2 + x_freq[None, None, :] ** 2
    safe = jnp.where(squared > 0, squared, 1.0)
    values = 4.0 * math.pi * (1.0 - jnp.exp(-safe / (4.0 * screening * screening))) / safe
    return jnp.where(squared > 0, values, math.pi / (screening * screening))


def reference(orbitals, partners, counts):
    depth, height, width = orbitals.shape[1], orbitals.shape[2], orbitals.shape[3]
    kernel = screened_kernel(frequency(depth, 0, depth), frequency(height, 0, height), frequency(width, 0, width // 2 + 1))

    def one_target(target_row):
        band = (target_row // TGT) * OWN + target_row % TGT
        target = lax.dynamic_index_in_dim(orbitals, band, 0, keepdims=False).astype(jnp.float32)

        def add_pair(slot, total):
            partner_band = partners[target_row, slot].astype(jnp.int32)
            partner = lax.dynamic_index_in_dim(orbitals, partner_band, 0, keepdims=False).astype(jnp.float32)
            density = target * partner
            potential = jnp.fft.irfftn(kernel * jnp.fft.rfftn(density), s=density.shape)
            weight = (slot < counts[target_row]).astype(jnp.float32)
            return total + weight * (potential * partner)

        start = jnp.zeros((depth, height, width), jnp.float32)
        return lax.fori_loop(0, PART, add_pair, start)

    return lax.map(one_target, jnp.arange(TARGETS, dtype=jnp.int32))
```

```python
import functools
import math

import jax
import jax.numpy as jnp
import ml_dtypes
import numpy as np
from jax import lax
from jax.experimental import pallas as pl
from jax.experimental.pallas import tpu as pltpu
from jax.sharding import PartitionSpec as P

screening = 0.032
MESH = pl.DeviceIdType.MESH
f32 = jnp.float32
bf16 = jnp.bfloat16


def frequency(length, start, count):
    index = start + jnp.arange(count, dtype=jnp.int32)
    folded = jnp.minimum(index, length - index).astype(f32)
    return 2.0 * math.pi / length * folded


def screened_kernel(z_freq, y_freq, x_freq):
    squared = z_freq[None, :, None] ** 2 + y_freq[:, None, None] ** 2 + x_freq[None, None, :] ** 2
    safe = jnp.where(squared > 0, squared, 1.0)
    values = 4.0 * math.pi * (1.0 - jnp.exp(-safe / (4.0 * screening * screening))) / safe
    return jnp.where(squared > 0, values, math.pi / (screening * screening))


def cas_table(length):
    index = np.arange(length)
    phase = (np.outer(index, index) % length) * (2.0 * np.pi / length)
    return np.cos(phase) + np.sin(phase)


def split_np(table):
    high = table.astype(ml_dtypes.bfloat16)
    low = (table - high.astype(np.float64)).astype(ml_dtypes.bfloat16)
    return high, low


def left_table(table):
    high, low = split_np(table)
    return np.concatenate([high, high, low], axis=1)


def tables(height, total, tiles, rows):
    cas = cas_table(height)
    swap = np.arange(height).reshape(-1, 2, rows)[:, ::-1].reshape(-1)
    cas_z = cas_table(total)
    order = np.arange(total)
    order = rows * (order % tiles) + order // tiles
    left = np.stack(
        [
            left_table(cas),
            left_table(cas[swap]),
            left_table(cas_z[:, order]),
            left_table(cas_z[order]),
            left_table(cas),
            left_table(cas[:, swap]),
        ]
    )
    high, low = split_np(cas)
    return left, np.concatenate([high, high, low], axis=0)


def split(value):
    high = value.astype(bf16)
    low = (value - high.astype(f32)).astype(bf16)
    return high, low


def times_right(value, table):
    high, low = split(value)
    return jnp.dot(jnp.concatenate([high, low, high], axis=1), table, preferred_element_type=f32)


def times_left(table, value):
    high, low = split(value)
    return jnp.dot(table, jnp.concatenate([high, low, high], axis=0), preferred_element_type=f32)


def exchange_kernel(
    cfg,
    index_ref,
    weight_ref,
    orb_ref,
    left_ref,
    right_ref,
    kern_ref,
    out_ref,
    held0,
    held1,
    held2,
    held3,
    send1,
    recv1,
    send2,
    recv2,
    own_sem,
    ring_send,
    ring_recv,
    s1_sem,
    r1_sem,
    s2_sem,
    r2_sem,
    l1_sem,
    l2_sem,
):
    groups, tiles, own, tgt, chunks, per = cfg
    held = (held0, held1, held2, held3)
    rows = len(held)
    half = own // 2
    me_b = lax.axis_index("band")
    me = lax.axis_index("grid")
    up = lax.rem(me_b + 1, groups)
    down = lax.rem(me_b + groups - 1, groups)

    barrier = pltpu.get_barrier_semaphore()
    for neighbour in (up, down):
        pl.semaphore_signal(barrier, inc=1, device_id=(neighbour, me), device_id_type=MESH)

    @pl.loop(1, tiles)
    def _(i):
        pl.semaphore_signal(
            barrier, inc=1, device_id=(me_b, lax.rem(me + i, tiles)), device_id_type=MESH
        )

    copies = []
    for r in range(rows):
        copy = pltpu.make_async_copy(
            orb_ref.at[:, r], held[r].at[pl.ds(me_b * own, own)], own_sem.at[r]
        )
        copy.start()
        copies.append(copy)
    pl.semaphore_wait(barrier, tiles + 1)
    for copy in copies:
        copy.wait()

    def ring(r, e, way):
        step = e // 2
        part = e % 2 if e < 6 else way
        if way == 0:
            block = lax.rem(me_b - step + groups, groups)
        else:
            block = lax.rem(me_b + step, groups)
        ref = held[r].at[pl.ds(block * own + part * half, half)]
        return pltpu.make_async_remote_copy(
            src_ref=ref,
            dst_ref=ref,
            send_sem=ring_send.at[way, r],
            recv_sem=ring_recv.at[way, r, e],
            device_id=(up if way == 0 else down, me),
            device_id_type=MESH,
        )

    def arrived(r, e, way):
        step = e // 2 + 1
        part = e % 2 if e < 6 else way
        if way == 0:
            block = lax.rem(me_b - step + groups, groups)
        else:
            block = lax.rem(me_b + step, groups)
        ref = held[r].at[pl.ds(block * own + part * half, half)]
        pltpu.make_async_copy(ref, ref, ring_recv.at[way, r, e]).wait()

    def before(e, way):
        return e - 2 if e < 6 else 4 + way

    def event(r, e):
        for way in range(2):
            if e >= 2:
                arrived(r, before(e, way), way)
            ring(r, e, way).start()

    def leftovers(r):
        for way in range(2):
            arrived(r, 5 - way, way)
            arrived(r, 6, way)

    low_rows = lax.broadcasted_iota(jnp.int32, (8, 128), 0) < 4

    def forward(r, c):
        @pl.loop(0, per)
        def _(k):
            pair = 2 * (c * per + k)
            turned = []
            for s in range(2):
                target = held[r][index_ref[0, pair + s]].astype(f32)
                partner = held[r][index_ref[1, pair + s]].astype(f32)
                along_x = times_right(target * partner, right_ref[...])
                turned.append(times_left(left_ref[s], along_x))
            first, second = turned
            for t in range(16):
                a, b = first[8 * t : 8 * t + 8], second[8 * t : 8 * t + 8]
                at = ((c * tiles + 2 * t) * per + k) * 8
                send1[r, pl.ds(pl.multiple_of(at, 8), 8)] = jnp.where(low_rows, a, b)
                at = ((c * tiles + 2 * t + 1) * per + k) * 8
                send1[r, pl.ds(pl.multiple_of(at, 8), 8)] = jnp.where(low_rows, b, a)

        size = per * 8

        @pl.loop(1, tiles)
        def _(i):
            to = lax.rem(me + i, tiles)
            pltpu.make_async_remote_copy(
                src_ref=send1.at[r, pl.ds(pl.multiple_of((c * tiles + to) * size, 8), size)],
                dst_ref=recv1.at[r, pl.ds(pl.multiple_of((c * tiles + me) * size, 8), size)],
                send_sem=s1_sem.at[r, c],
                recv_sem=r1_sem.at[r, c],
                device_id=(me_b, to),
                device_id_type=MESH,
            ).start()

        at = pl.ds(pl.multiple_of((c * tiles + me) * size, 8), size)
        pltpu.make_async_copy(send1.at[r, at], recv1.at[r, at], r1_sem.at[r, c]).start()

    def turn(c):
        for r in range(rows):
            at = pl.ds(c * tiles * per * 8, tiles * per * 8)
            pltpu.make_async_copy(recv1.at[r, at], recv1.at[r, at], r1_sem.at[r, c]).wait()

        @pl.loop(0, per)
        def _(k):
            for q in range(0, 8, 2):
                columns = []
                for p in (q, q + 1):
                    columns.append(
                        jnp.concatenate(
                            [
                                recv1[r, pl.ds((c * tiles * per + k) * 8 + p, tiles, stride=per * 8)]
                                for r in range(rows)
                            ],
                            axis=0,
                        )
                    )
                image = times_left(left_ref[2], jnp.concatenate(columns, axis=1))
                image = image * jnp.concatenate([kern_ref[q % 4], kern_ref[q % 4 + 1]], axis=1)
                back = times_left(left_ref[3], image)
                for p in range(2):
                    for r in range(rows):
                        send2[
                            pl.ds(((c * tiles * per + k) * rows + r) * 8 + q + p, tiles, stride=per * rows * 8)
                        ] = back[r * tiles : (r + 1) * tiles, p * 128 : (p + 1) * 128]

        size = per * rows * 8

        @pl.loop(1, tiles)
        def _(i):
            to = lax.rem(me + i, tiles)
            pltpu.make_async_remote_copy(
                src_ref=send2.at[pl.ds(pl.multiple_of((c * tiles + to) * size, 8), size)],
                dst_ref=recv2.at[pl.ds(pl.multiple_of((c * tiles + me) * size, 8), size)],
                send_sem=s2_sem.at[c],
                recv_sem=r2_sem.at[c],
                device_id=(me_b, to),
                device_id_type=MESH,
            ).start()

        at = pl.ds(pl.multiple_of((c * tiles + me) * size, 8), size)
        pltpu.make_async_copy(send2.at[at], recv2.at[at], r2_sem.at[c]).start()

    def backward(c):
        at = pl.ds(c * tiles * per * rows * 8, tiles * per * rows * 8)
        pltpu.make_async_copy(recv2.at[at], recv2.at[at], r2_sem.at[c]).wait()

        @pl.loop(0, per)
        def _(k):
            pair = 2 * (c * per + k)
            for r in range(rows):
                pieces = []
                for s in range(tiles):
                    row = (((c * tiles + s) * per + k) * rows + r) * 8
                    pieces.append(recv2[pl.ds(pl.multiple_of(row, 8), 8)])
                waves = (
                    jnp.concatenate([jnp.where(low_rows, pieces[2 * t], pieces[2 * t + 1]) for t in range(16)], axis=0),
                    jnp.concatenate([jnp.where(low_rows, pieces[2 * t + 1], pieces[2 * t]) for t in range(16)], axis=0),
                )
                terms = []
                for s in range(2):
                    potential = times_right(times_left(left_ref[4 + s], waves[s]), right_ref[...])
                    terms.append(potential * held[r][index_ref[1, pair + s]].astype(f32))
                for j in range(tgt):
                    out_ref[j, r] += (
                        weight_ref[j, pair] * terms[0] + weight_ref[j, pair + 1] * terms[1]
                    )

    out_ref[...] = jnp.zeros_like(out_ref)
    shares = [[] for _ in range(7)]
    for c in range(chunks):
        shares[2 + c * 5 // chunks].append(c)
    for r in range(rows):
        for e in range(7):
            event(r, e)
            if r > 0:
                if e == 1:
                    leftovers(r - 1)
                for c in shares[e]:
                    forward(r - 1, c)
    leftovers(rows - 1)
    for c in range(chunks):
        forward(rows - 1, c)
    for c in range(chunks):
        turn(c)
    for c in range(chunks):
        backward(c)

    for way in range(2):
        for r in range(rows):
            ref = held[r].at[pl.ds(0, 7 * half)]
            pltpu.make_async_copy(ref, ref, ring_send.at[way, r]).wait()
    for c in range(chunks):
        for r in range(rows):
            ref = send1.at[r, pl.ds(0, (tiles - 1) * per * 8)]
            pltpu.make_async_copy(ref, ref, s1_sem.at[r, c]).wait()
        ref = send2.at[pl.ds(0, (tiles - 1) * per * rows * 8)]
        pltpu.make_async_copy(ref, ref, s2_sem.at[c]).wait()


SHAPES = {24: (4, 3)}


def run_exchange(slots, orbitals, index, weight, kern, left, right, groups, tiles, tgt):
    own, rows, height, width = orbitals.shape
    chunks, per = SHAPES[slots]
    total = chunks * tiles * per * 8
    vmem = pl.BlockSpec(memory_space=pltpu.VMEM)
    smem = pl.BlockSpec(memory_space=pltpu.SMEM)
    return pl.pallas_call(
        functools.partial(exchange_kernel, (groups, tiles, own, tgt, chunks, per)),
        out_shape=jax.ShapeDtypeStruct((tgt, rows, height, width), f32),
        in_specs=[smem, smem, pl.BlockSpec(memory_space=pl.ANY), vmem, vmem, vmem],
        out_specs=vmem,
        scratch_shapes=[pltpu.VMEM((groups * own, height, width), bf16)] * rows
        + [
            pltpu.VMEM((rows, total, width), f32),
            pltpu.VMEM((rows, total, width), f32),
            pltpu.VMEM((total * rows, width), f32),
            pltpu.VMEM((total * rows, width), f32),
            pltpu.SemaphoreType.DMA((rows,)),
            pltpu.SemaphoreType.DMA((2, rows)),
            pltpu.SemaphoreType.DMA((2, rows, 7)),
            pltpu.SemaphoreType.DMA((rows, chunks)),
            pltpu.SemaphoreType.DMA((rows, chunks)),
            pltpu.SemaphoreType.DMA((chunks,)),
            pltpu.SemaphoreType.DMA((chunks,)),
            pltpu.SemaphoreType.DMA,
            pltpu.SemaphoreType.DMA,
        ],
        compiler_params=pltpu.CompilerParams(
            collective_id=slots, has_side_effects=True, vmem_limit_bytes=60 * 1024 * 1024
        ),
    )(index, weight, orbitals, left, right, kern)


def pair_lists(partners, counts, band_index, tgt, own, slots):
    part = partners.shape[1]
    own_lists = lax.dynamic_slice_in_dim(partners, band_index * tgt, tgt, 0)
    own_counts = lax.dynamic_slice_in_dim(counts, band_index * tgt, tgt, 0)
    slot = jnp.arange(part, dtype=jnp.int32)
    active = (slot[None, :] < own_counts[:, None]).reshape(-1)
    every = jnp.arange(tgt * part, dtype=jnp.int32)
    place = jnp.sum(((every[None, :] < every[:, None]) & active[None, :]).astype(jnp.int32), axis=1)
    chosen = active[None, :] & (place[None, :] == jnp.arange(slots, dtype=jnp.int32)[:, None])
    partner = jnp.sum(jnp.where(chosen, own_lists.reshape(-1)[None, :], 0), axis=1)
    which = jnp.sum(jnp.where(chosen, (every // part)[None, :], 0), axis=1)
    target = band_index * own + which
    live = jnp.any(chosen, axis=1)
    weight = ((which[None, :] == jnp.arange(tgt)[:, None]) & live[None, :]).astype(f32)
    return jnp.stack([target, partner]), weight


def per_device(orbitals, partners, counts):
    own, depth, height, width = orbitals.shape
    groups = lax.axis_size("band")
    tiles = lax.axis_size("grid")
    total_depth = depth * tiles
    band_index = lax.axis_index("band")
    tgt = partners.shape[0] // groups
    slab_rows = height // tiles
    kernel = screened_kernel(
        frequency(total_depth, 0, total_depth),
        frequency(height, lax.axis_index("grid") * slab_rows, slab_rows),
        frequency(width, 0, width),
    )
    kernel = kernel / float(total_depth * height * width)
    left, right = tables(height, total_depth, tiles, depth)
    slots = 24
    index, weight = pair_lists(partners, counts, band_index, tgt, own, slots)
    return run_exchange(
        slots, orbitals, index, weight, kernel, jnp.asarray(left), jnp.asarray(right), groups, tiles, tgt
    )


def solution(mesh):
    return jax.shard_map(
        per_device,
        mesh=mesh,
        in_specs=(P("band", "grid", None, None), P(), P()),
        out_specs=P("band", "grid", None, None),
        check_vma=False,
    )
```

```python
import functools
import math

import jax
import jax.numpy as jnp
import ml_dtypes
import numpy as np
from jax import lax
from jax.experimental import pallas as pl
from jax.experimental.pallas import tpu as pltpu
from jax.sharding import PartitionSpec as P

screening = 0.032
MESH = pl.DeviceIdType.MESH
f32 = jnp.float32
bf16 = jnp.bfloat16


def frequency(length, start, count):
    index = start + jnp.arange(count, dtype=jnp.int32)
    folded = jnp.minimum(index, length - index).astype(f32)
    return 2.0 * math.pi / length * folded


def screened_kernel(z_freq, y_freq, x_freq):
    squared = z_freq[None, :, None] ** 2 + y_freq[:, None, None] ** 2 + x_freq[None, None, :] ** 2
    safe = jnp.where(squared > 0, squared, 1.0)
    values = 4.0 * math.pi * (1.0 - jnp.exp(-safe / (4.0 * screening * screening))) / safe
    return jnp.where(squared > 0, values, math.pi / (screening * screening))


def cas_table(length):
    index = np.arange(length)
    phase = (np.outer(index, index) % length) * (2.0 * np.pi / length)
    return np.cos(phase) + np.sin(phase)


def split_np(table):
    high = table.astype(ml_dtypes.bfloat16)
    low = (table - high.astype(np.float64)).astype(ml_dtypes.bfloat16)
    return high, low


def left_table(table):
    high, low = split_np(table)
    return np.concatenate([high, high, low], axis=1)


def tables(height, total, tiles, rows):
    cas = cas_table(height)
    swap = np.arange(height).reshape(-1, 2, rows)[:, ::-1].reshape(-1)
    cas_z = cas_table(total)
    order = np.arange(total)
    order = rows * (order % tiles) + order // tiles
    left = np.stack(
        [
            left_table(cas),
            left_table(cas[swap]),
            left_table(cas_z[:, order]),
            left_table(cas_z[order]),
            left_table(cas),
            left_table(cas[:, swap]),
        ]
    )
    high, low = split_np(cas)
    return left, np.concatenate([high, high, low], axis=0)


def split(value):
    high = value.astype(bf16)
    low = (value - high.astype(f32)).astype(bf16)
    return high, low


def times_right(value, table):
    high, low = split(value)
    return jnp.dot(jnp.concatenate([high, low, high], axis=1), table, preferred_element_type=f32)


def times_left(table, value):
    high, low = split(value)
    return jnp.dot(table, jnp.concatenate([high, low, high], axis=0), preferred_element_type=f32)


def regions(caps, own):
    first, table = own, []
    for _ in range(2):
        row = []
        for cap in (caps[0],) + tuple(caps):
            row.append(first)
            first += cap
        table.append(row)
    return table, first


def exchange_kernel(
    cfg,
    index_ref,
    order_ref,
    weight_ref,
    orb_ref,
    left_ref,
    right_ref,
    kern_ref,
    out_ref,
    held0,
    held1,
    held2,
    held3,
    stage,
    send1,
    recv1,
    send2,
    recv2,
    own_sem,
    ring_send,
    ring_recv,
    s1_sem,
    r1_sem,
    s2_sem,
    r2_sem,
):
    groups, tiles, own, tgt, chunks, per, caps = cfg
    held = (held0, held1, held2, held3)
    rows = len(held)
    first, _ = regions(caps, own)
    me_b = lax.axis_index("band")
    me = lax.axis_index("grid")
    up = lax.rem(me_b + 1, groups)
    down = lax.rem(me_b + groups - 1, groups)

    fetch = pltpu.make_async_copy(orb_ref, stage, own_sem)
    fetch.start()
    barrier = pltpu.get_barrier_semaphore()
    for neighbour in (up, down):
        pl.semaphore_signal(barrier, inc=1, device_id=(neighbour, me), device_id_type=MESH)

    @pl.loop(1, tiles)
    def _(i):
        pl.semaphore_signal(
            barrier, inc=1, device_id=(me_b, lax.rem(me + i, tiles)), device_id_type=MESH
        )

    fetch.wait()
    for r in range(rows):
        for way in range(2):

            @pl.loop(0, caps[0])
            def _(s):
                held[r][first[way][0] + s] = stage[order_ref[way, s], r]

    pl.semaphore_wait(barrier, tiles + 1)

    def span(e):
        hop = e // 2
        cut = (caps[hop] + 1) // 2
        if e == 6:
            return hop, 0, caps[hop]
        return (hop, 0, cut) if e % 2 == 0 else (hop, cut, caps[hop])

    def event(r, e):
        hop, start, end = span(e)
        for way in range(2):
            if e >= 2:
                arrived(r, e - 2, way)
            pltpu.make_async_remote_copy(
                src_ref=held[r].at[pl.ds(first[way][hop] + start, end - start)],
                dst_ref=held[r].at[pl.ds(first[way][hop + 1] + start, end - start)],
                send_sem=ring_send.at[way, r],
                recv_sem=ring_recv.at[way, r, e],
                device_id=(down if way else up, me),
                device_id_type=MESH,
            ).start()

    def arrived(r, e, way):
        hop, start, end = span(e)
        ref = held[r].at[pl.ds(first[way][hop + 1] + start, end - start)]
        pltpu.make_async_copy(ref, ref, ring_recv.at[way, r, e]).wait()

    def leftovers(r):
        for way in range(2):
            arrived(r, 5, way)
            arrived(r, 6, way)

    low_rows = lax.broadcasted_iota(jnp.int32, (8, 128), 0) < 4

    def forward(r, c):
        @pl.loop(0, per)
        def _(k):
            pair = 2 * (c * per + k)
            turned = []
            for s in range(2):
                target = held[r][index_ref[0, pair + s]].astype(f32)
                partner = held[r][index_ref[1, pair + s]].astype(f32)
                along_x = times_right(target * partner, right_ref[...])
                turned.append(times_left(left_ref[s], along_x))
            one, two = turned
            for t in range(16):
                a, b = one[8 * t : 8 * t + 8], two[8 * t : 8 * t + 8]
                at = ((c * tiles + 2 * t) * per + k) * 8
                send1[r, pl.ds(pl.multiple_of(at, 8), 8)] = jnp.where(low_rows, a, b)
                at = ((c * tiles + 2 * t + 1) * per + k) * 8
                send1[r, pl.ds(pl.multiple_of(at, 8), 8)] = jnp.where(low_rows, b, a)

        size = per * 8

        @pl.loop(1, tiles)
        def _(i):
            to = lax.rem(me + i, tiles)
            pltpu.make_async_remote_copy(
                src_ref=send1.at[r, pl.ds(pl.multiple_of((c * tiles + to) * size, 8), size)],
                dst_ref=recv1.at[r, pl.ds(pl.multiple_of((c * tiles + me) * size, 8), size)],
                send_sem=s1_sem.at[r, c],
                recv_sem=r1_sem.at[r, c],
                device_id=(me_b, to),
                device_id_type=MESH,
            ).start()

        at = pl.ds(pl.multiple_of((c * tiles + me) * size, 8), size)
        pltpu.make_async_copy(send1.at[r, at], recv1.at[r, at], r1_sem.at[r, c]).start()

    def turn(c):
        for r in range(rows):
            at = pl.ds(pl.multiple_of(c * tiles * per * 8, 8), tiles * per * 8)
            pltpu.make_async_copy(recv1.at[r, at], recv1.at[r, at], r1_sem.at[r, c]).wait()

        @pl.loop(0, per)
        def _(k):
            for q in range(0, 8, 2):
                columns = []
                for p in (q, q + 1):
                    columns.append(
                        jnp.concatenate(
                            [
                                recv1[r, pl.ds((c * tiles * per + k) * 8 + p, tiles, stride=per * 8)]
                                for r in range(rows)
                            ],
                            axis=0,
                        )
                    )
                image = times_left(left_ref[2], jnp.concatenate(columns, axis=1))
                image = image * jnp.concatenate([kern_ref[q % 4], kern_ref[q % 4 + 1]], axis=1)
                back = times_left(left_ref[3], image)
                for p in range(2):
                    for r in range(rows):
                        send2[
                            pl.ds(((c * tiles * per + k) * rows + r) * 8 + q + p, tiles, stride=per * rows * 8)
                        ] = back[r * tiles : (r + 1) * tiles, p * 128 : (p + 1) * 128]

        size = per * rows * 8

        @pl.loop(1, tiles)
        def _(i):
            to = lax.rem(me + i, tiles)
            pltpu.make_async_remote_copy(
                src_ref=send2.at[pl.ds(pl.multiple_of((c * tiles + to) * size, 8), size)],
                dst_ref=recv2.at[pl.ds(pl.multiple_of((c * tiles + me) * size, 8), size)],
                send_sem=s2_sem.at[c],
                recv_sem=r2_sem.at[c],
                device_id=(me_b, to),
                device_id_type=MESH,
            ).start()

        at = pl.ds(pl.multiple_of((c * tiles + me) * size, 8), size)
        pltpu.make_async_copy(send2.at[at], recv2.at[at], r2_sem.at[c]).start()

    def backward(c):
        at = pl.ds(pl.multiple_of(c * tiles * per * rows * 8, 8), tiles * per * rows * 8)
        pltpu.make_async_copy(recv2.at[at], recv2.at[at], r2_sem.at[c]).wait()

        @pl.loop(0, per)
        def _(k):
            pair = 2 * (c * per + k)
            for r in range(rows):
                pieces = []
                for s in range(tiles):
                    row = (((c * tiles + s) * per + k) * rows + r) * 8
                    pieces.append(recv2[pl.ds(pl.multiple_of(row, 8), 8)])
                waves = (
                    jnp.concatenate([jnp.where(low_rows, pieces[2 * t], pieces[2 * t + 1]) for t in range(16)], axis=0),
                    jnp.concatenate([jnp.where(low_rows, pieces[2 * t + 1], pieces[2 * t]) for t in range(16)], axis=0),
                )
                terms = []
                for s in range(2):
                    potential = times_right(times_left(left_ref[4 + s], waves[s]), right_ref[...])
                    terms.append(potential * held[r][index_ref[1, pair + s]].astype(f32))
                for j in range(tgt):
                    out_ref[j, r] += (
                        weight_ref[j, pair] * terms[0] + weight_ref[j, pair + 1] * terms[1]
                    )

    def keep(r):
        for i in range(own):
            held[r][i] = stage[i, r]

    for r in range(rows):
        event(r, 0)
        event(r, 1)
        if r == 0:
            for q in range(rows):
                keep(q)
            out_ref[...] = jnp.zeros_like(out_ref)
            for e in range(2, 7):
                event(r, e)
        else:
            leftovers(r - 1)

            @pl.loop(0, 5)
            def _(step):
                for e in range(2, 7):
                    pl.when(step == e - 2)(functools.partial(event, r, e))
                pl.when(step < chunks)(functools.partial(forward, r - 1, step))

    leftovers(rows - 1)
    pl.loop(0, chunks)(functools.partial(forward, rows - 1))
    pl.loop(0, chunks)(turn)
    pl.loop(0, chunks)(backward)

    for way in range(2):
        for r in range(rows):
            ref = held[r].at[pl.ds(0, sum(caps))]
            pltpu.make_async_copy(ref, ref, ring_send.at[way, r]).wait()
    for c in range(chunks):
        for r in range(rows):
            ref = send1.at[r, pl.ds(0, (tiles - 1) * per * 8)]
            pltpu.make_async_copy(ref, ref, s1_sem.at[r, c]).wait()
        ref = send2.at[pl.ds(0, (tiles - 1) * per * rows * 8)]
        pltpu.make_async_copy(ref, ref, s2_sem.at[c]).wait()


def run_exchange(slots, chunks, caps, tiles, orbitals, index, order, weight, kern, left, right):
    own, rows, height, width = orbitals.shape
    tgt = weight.shape[0]
    per = slots // 2 // chunks
    total = chunks * tiles * per * 8
    room = regions(caps, own)[1]
    vmem = pl.BlockSpec(memory_space=pltpu.VMEM)
    smem = pl.BlockSpec(memory_space=pltpu.SMEM)
    groups = lax.axis_size("band")
    return pl.pallas_call(
        functools.partial(exchange_kernel, (groups, tiles, own, tgt, chunks, per, caps)),
        out_shape=jax.ShapeDtypeStruct((tgt, rows, height, width), f32),
        in_specs=[smem, smem, smem, pl.BlockSpec(memory_space=pl.ANY), vmem, vmem, vmem],
        out_specs=vmem,
        scratch_shapes=[pltpu.VMEM((room, height, width), bf16)] * rows
        + [
            pltpu.VMEM((own, rows, height, width), bf16),
            pltpu.VMEM((rows, total, width), f32),
            pltpu.VMEM((rows, total, width), f32),
            pltpu.VMEM((total * rows, width), f32),
            pltpu.VMEM((total * rows, width), f32),
            pltpu.SemaphoreType.DMA,
            pltpu.SemaphoreType.DMA((2, rows)),
            pltpu.SemaphoreType.DMA((2, rows, 7)),
            pltpu.SemaphoreType.DMA((rows, chunks)),
            pltpu.SemaphoreType.DMA((rows, chunks)),
            pltpu.SemaphoreType.DMA((chunks,)),
            pltpu.SemaphoreType.DMA((chunks,)),
        ],
        compiler_params=pltpu.CompilerParams(
            collective_id=slots, has_side_effects=True, vmem_limit_bytes=60 * 1024 * 1024
        ),
    )(index, order, weight, orbitals, left, right, kern)


def routes(partners, counts, groups, tgt, own):
    targets, part = partners.shape
    active = jnp.arange(part, dtype=jnp.int32)[None, :] < counts[:, None]
    home = jnp.arange(targets, dtype=jnp.int32)[:, None] // tgt
    hop = (home - partners // own + groups) % groups
    code = jnp.where(active, partners * groups + hop, -1).reshape(-1)
    every = jnp.arange(groups * own * groups, dtype=jnp.int32)
    need = jnp.any(code[:, None] == every[None, :], axis=0).reshape(groups, own, groups)
    up3 = jnp.where(need[:, :, 3], 3, jnp.where(need[:, :, 2], 2, need[:, :, 1].astype(jnp.int32)))
    down3 = jnp.where(need[:, :, 5], 3, jnp.where(need[:, :, 6], 2, need[:, :, 7].astype(jnp.int32)))
    opposite = need[:, :, 4]
    lane = jnp.arange(own, dtype=jnp.int32)

    def place(key):
        full = key * own + lane[None, :]
        return jnp.sum((full[:, None, :] < full[:, :, None]).astype(jnp.int32), axis=2)

    turn = place(jnp.where(opposite, down3 - up3, 100))
    halfway = (jnp.sum(opposite.astype(jnp.int32), axis=1, keepdims=True) + 1) // 2
    goes_up = opposite & (turn < halfway)
    far = jnp.stack([jnp.where(goes_up, 4, up3), jnp.where(opposite & ~goes_up, 4, down3)])
    ranks = jnp.stack([place(-far[0]), place(-far[1])])
    hops = jnp.arange(1, 5, dtype=jnp.int32)
    load = jnp.max(jnp.sum((far[..., None] >= hops).astype(jnp.int32), axis=2), axis=(0, 1))
    return ranks, goes_up, load


def pair_lists(partners, counts, ranks, goes_up, band_index, groups, tgt, own, slots):
    part = partners.shape[1]
    own_lists = lax.dynamic_slice_in_dim(partners, band_index * tgt, tgt, 0).reshape(-1)
    own_counts = lax.dynamic_slice_in_dim(counts, band_index * tgt, tgt, 0)
    slot = jnp.arange(part, dtype=jnp.int32)
    active = (slot[None, :] < own_counts[:, None]).reshape(-1)
    every = jnp.arange(tgt * part, dtype=jnp.int32)
    place = jnp.sum(((every[None, :] < every[:, None]) & active[None, :]).astype(jnp.int32), axis=1)
    chosen = active[None, :] & (place[None, :] == jnp.arange(slots, dtype=jnp.int32)[:, None])
    partner = jnp.sum(jnp.where(chosen, own_lists[None, :], 0), axis=1)
    which = jnp.sum(jnp.where(chosen, (every // part)[None, :], 0), axis=1)
    live = jnp.any(chosen, axis=1)
    weight = ((which[None, :] == jnp.arange(tgt)[:, None]) & live[None, :]).astype(f32)
    hop = (band_index - partner // own + groups) % groups
    band = partner[:, None] == jnp.arange(groups * own, dtype=jnp.int32)[None, :]
    rises = jnp.any(band & goes_up.reshape(1, -1), axis=1)
    way = ((hop > 4) | ((hop == 4) & ~rises)).astype(jnp.int32)
    rank = jnp.sum(jnp.where(band, jnp.where(way[:, None] > 0, ranks[1].reshape(1, -1), ranks[0].reshape(1, -1)), 0), axis=1)
    far = jnp.where(live, jnp.where(hop > 4, groups - hop, hop), 0)
    return which, partner % own, way, far, rank, weight


VARIANTS = (
    (16, 4, (7, 6, 5, 2)),
    (18, 3, (7, 6, 5, 2)),
    (20, 5, (8, 7, 6, 3)),
    (24, 4, (8, 8, 8, 4)),
)


def per_device(orbitals, partners, counts):
    own, depth, height, width = orbitals.shape
    groups = lax.axis_size("band")
    tiles = lax.axis_size("grid")
    total_depth = depth * tiles
    band_index = lax.axis_index("band")
    tgt = partners.shape[0] // groups
    slab_rows = height // tiles
    kernel = screened_kernel(
        frequency(total_depth, 0, total_depth),
        frequency(height, lax.axis_index("grid") * slab_rows, slab_rows),
        frequency(width, 0, width),
    )
    kernel = kernel / float(total_depth * height * width)
    left, right = tables(height, total_depth, tiles, depth)
    ranks, goes_up, load = routes(partners, counts, groups, tgt, own)
    most = jnp.max(jnp.sum(counts.reshape(groups, tgt), axis=1))
    slots = VARIANTS[-1][0]
    which, local, way, far, rank, weight = pair_lists(
        partners, counts, ranks, goes_up, band_index, groups, tgt, own, slots
    )
    own_ranks = lax.dynamic_slice_in_dim(ranks, band_index, 1, 1)[:, 0]
    lane = jnp.arange(own, dtype=jnp.int32)
    order = jnp.sum(jnp.where(own_ranks[:, None, :] == lane[None, :, None], lane[None, None, :], 0), axis=2)
    pick = jnp.int32(len(VARIANTS) - 1)
    for at in reversed(range(len(VARIANTS) - 1)):
        some, _, caps = VARIANTS[at]
        pick = jnp.where((most <= some) & jnp.all(load <= jnp.array(caps, jnp.int32)), at, pick)

    def branch(variant):
        some, chunks, caps = variant
        table, _ = regions(caps, own)

        def run(orbitals, which, local, way, far, rank, weight, order, kernel, left, right):
            slot = jnp.zeros_like(far)
            for w in range(2):
                for h in range(1, 5):
                    slot = jnp.where((way == w) & (far == h), table[w][h] + rank, slot)
            slot = jnp.where(far == 0, local, slot)
            index = jnp.stack([which, slot])[:, :some]
            return run_exchange(
                some, chunks, caps, tiles, orbitals, index, order, weight[:, :some], kernel, left, right
            )

        return run

    return lax.switch(
        pick,
        [branch(v) for v in VARIANTS],
        orbitals, which, local, way, far, rank, weight, order, kernel, jnp.asarray(left), jnp.asarray(right),
    )


def solution(mesh):
    return jax.shard_map(
        per_device,
        mesh=mesh,
        in_specs=(P("band", "grid", None, None), P(), P()),
        out_specs=P("band", "grid", None, None),
        check_vma=False,
    )
```

```python
import functools
import math

import jax
import jax.numpy as jnp
import ml_dtypes
import numpy as np
from jax import lax
from jax.experimental import pallas as pl
from jax.experimental.pallas import tpu as pltpu
from jax.sharding import PartitionSpec as P

screening = 0.032
MESH = pl.DeviceIdType.MESH
f32 = jnp.float32
bf16 = jnp.bfloat16


def frequency(length, start, count):
    index = start + jnp.arange(count, dtype=jnp.int32)
    folded = jnp.minimum(index, length - index).astype(f32)
    return 2.0 * math.pi / length * folded


def screened_kernel(z_freq, y_freq, x_freq):
    squared = z_freq[None, :, None] ** 2 + y_freq[:, None, None] ** 2 + x_freq[None, None, :] ** 2
    safe = jnp.where(squared > 0, squared, 1.0)
    values = 4.0 * math.pi * (1.0 - jnp.exp(-safe / (4.0 * screening * screening))) / safe
    return jnp.where(squared > 0, values, math.pi / (screening * screening))


def cas_table(length):
    index = np.arange(length)
    phase = (np.outer(index, index) % length) * (2.0 * np.pi / length)
    return np.cos(phase) + np.sin(phase)


def split_np(table):
    high = table.astype(ml_dtypes.bfloat16)
    low = (table - high.astype(np.float64)).astype(ml_dtypes.bfloat16)
    return high, low


def left_table(table):
    high, low = split_np(table)
    return np.concatenate([high, high, low], axis=1)


def tables(height, total, tiles, rows):
    cas = cas_table(height)
    swap = np.arange(height).reshape(-1, 2, rows)[:, ::-1].reshape(-1)
    cas_z = cas_table(total)
    order = np.arange(total)
    order = rows * (order % tiles) + order // tiles
    left = np.stack(
        [
            left_table(cas),
            left_table(cas[swap]),
            left_table(cas_z[:, order]),
            left_table(cas_z[order]),
            left_table(cas),
            left_table(cas[:, swap]),
        ]
    )
    high, low = split_np(cas)
    return left, np.concatenate([high, high, low], axis=0)


def split(value):
    high = value.astype(bf16)
    low = (value - high.astype(f32)).astype(bf16)
    return high, low


def times_right(value, table):
    high, low = split(value)
    return jnp.dot(jnp.concatenate([high, low, high], axis=1), table, preferred_element_type=f32)


def times_left(table, value):
    high, low = split(value)
    return jnp.dot(table, jnp.concatenate([high, low, high], axis=0), preferred_element_type=f32)


def regions(caps, own):
    first, table = own, []
    for _ in range(2):
        row = []
        for cap in (caps[0],) + tuple(caps):
            row.append(first)
            first += cap
        table.append(row)
    return table, first


def exchange_kernel(
    cfg,
    index_ref,
    order_ref,
    weight_ref,
    orb_ref,
    left_ref,
    right_ref,
    kern_ref,
    out_ref,
    held0,
    held1,
    held2,
    held3,
    stage,
    send1,
    recv1,
    send2,
    recv2,
    plain,
    grain,
    scale_out,
    scale_in,
    own_sem,
    ring_send,
    ring_recv,
    s1_sem,
    r1_sem,
    s2_sem,
    r2_sem,
    s3_sem,
    r3_sem,
):
    groups, tiles, own, tgt, chunks, per, caps = cfg
    held = (held0, held1, held2, held3)
    rows = len(held)
    first, _ = regions(caps, own)
    me_b = lax.axis_index("band")
    me = lax.axis_index("grid")
    up = lax.rem(me_b + 1, groups)
    down = lax.rem(me_b + groups - 1, groups)

    fetch = pltpu.make_async_copy(orb_ref, stage, own_sem)
    fetch.start()
    barrier = pltpu.get_barrier_semaphore()
    for neighbour in (up, down):
        pl.semaphore_signal(barrier, inc=1, device_id=(neighbour, me), device_id_type=MESH)

    @pl.loop(1, tiles)
    def _(i):
        pl.semaphore_signal(
            barrier, inc=1, device_id=(me_b, lax.rem(me + i, tiles)), device_id_type=MESH
        )

    fetch.wait()
    for r in range(rows):
        for way in range(2):

            @pl.loop(0, caps[0])
            def _(s):
                held[r][first[way][0] + s] = stage[order_ref[way, s], r]

    pl.semaphore_wait(barrier, tiles + 1)

    def span(e):
        hop = e // 2
        cut = (caps[hop] + 1) // 2
        if e == 6:
            return hop, 0, caps[hop]
        return (hop, 0, cut) if e % 2 == 0 else (hop, cut, caps[hop])

    def event(r, e):
        hop, start, end = span(e)
        for way in range(2):
            if e >= 2:
                arrived(r, e - 2, way)
            pltpu.make_async_remote_copy(
                src_ref=held[r].at[pl.ds(first[way][hop] + start, end - start)],
                dst_ref=held[r].at[pl.ds(first[way][hop + 1] + start, end - start)],
                send_sem=ring_send.at[way, r],
                recv_sem=ring_recv.at[way, r, e],
                device_id=(down if way else up, me),
                device_id_type=MESH,
            ).start()

    def arrived(r, e, way):
        hop, start, end = span(e)
        ref = held[r].at[pl.ds(first[way][hop + 1] + start, end - start)]
        pltpu.make_async_copy(ref, ref, ring_recv.at[way, r, e]).wait()

    def leftovers(r):
        for way in range(2):
            arrived(r, 5, way)
            arrived(r, 6, way)

    low_rows = lax.broadcasted_iota(jnp.int32, (8, 128), 0) < 4

    def forward(r, c):
        @pl.loop(0, per)
        def _(k):
            pair = 2 * (c * per + k)
            turned = []
            for s in range(2):
                target = held[r][index_ref[0, pair + s]].astype(f32)
                partner = held[r][index_ref[1, pair + s]].astype(f32)
                along_x = times_right(target * partner, right_ref[...])
                turned.append(times_left(left_ref[s], along_x))
            one, two = turned
            for t in range(16):
                a, b = one[8 * t : 8 * t + 8], two[8 * t : 8 * t + 8]
                at = ((c * tiles + 2 * t) * per + k) * 8
                send1[r, pl.ds(pl.multiple_of(at, 8), 8)] = jnp.where(low_rows, a, b)
                at = ((c * tiles + 2 * t + 1) * per + k) * 8
                send1[r, pl.ds(pl.multiple_of(at, 8), 8)] = jnp.where(low_rows, b, a)

        size = per * 8

        @pl.loop(1, tiles)
        def _(i):
            to = lax.rem(me + i, tiles)
            pltpu.make_async_remote_copy(
                src_ref=send1.at[r, pl.ds(pl.multiple_of((c * tiles + to) * size, 8), size)],
                dst_ref=recv1.at[r, pl.ds(pl.multiple_of((c * tiles + me) * size, 8), size)],
                send_sem=s1_sem.at[r, c],
                recv_sem=r1_sem.at[r, c],
                device_id=(me_b, to),
                device_id_type=MESH,
            ).start()

        at = pl.ds(pl.multiple_of((c * tiles + me) * size, 8), size)
        pltpu.make_async_copy(send1.at[r, at], recv1.at[r, at], r1_sem.at[r, c]).start()

    def turn(c):
        for r in range(rows):
            at = pl.ds(pl.multiple_of(c * tiles * per * 8, 8), tiles * per * 8)
            pltpu.make_async_copy(recv1.at[r, at], recv1.at[r, at], r1_sem.at[r, c]).wait()

        @pl.loop(0, per)
        def _(k):
            tops = []
            for q in range(0, 8, 2):
                columns = []
                for p in (q, q + 1):
                    columns.append(
                        jnp.concatenate(
                            [
                                recv1[r, pl.ds((c * tiles * per + k) * 8 + p, tiles, stride=per * 8)]
                                for r in range(rows)
                            ],
                            axis=0,
                        )
                    )
                image = times_left(left_ref[2], jnp.concatenate(columns, axis=1))
                image = image * jnp.concatenate([kern_ref[q % 4], kern_ref[q % 4 + 1]], axis=1)
                back = times_left(left_ref[3], image)
                for p in range(2):
                    part = back[:, p * 128 : (p + 1) * 128]
                    top = jnp.max(jnp.abs(part), axis=0, keepdims=True)
                    if (q + p) % 4 == 0:
                        tops.append(top)
                    else:
                        tops[-1] = jnp.maximum(tops[-1], top)
                    for r in range(rows):
                        plain[pl.ds(r * 8 + q + p, tiles, stride=rows * 8)] = part[r * tiles : (r + 1) * tiles]
            tops = [jnp.maximum(top, 1e-30) for top in tops]
            for p in range(2):
                scale_out[c, pl.ds(2 * k + p, 1)] = tops[p] * (1.0 / 32766.0)
            fine = jnp.where(
                low_rows,
                jnp.broadcast_to(32766.0 / tops[0], (8, 128)),
                jnp.broadcast_to(32766.0 / tops[1], (8, 128)),
            )
            fine = jnp.concatenate([fine] * rows, axis=0)
            for t in range(tiles):
                coded = jnp.round(plain[rows * 8 * t : rows * 8 * (t + 1)] * fine)
                at = ((c * tiles + t) * per + k) * rows * 8
                send2[pl.ds(pl.multiple_of(at, rows * 8), rows * 8)] = coded.astype(jnp.int32).astype(jnp.int16)

        size = per * rows * 8

        @pl.loop(1, tiles)
        def _(i):
            to = lax.rem(me + i, tiles)
            pltpu.make_async_remote_copy(
                src_ref=scale_out.at[c],
                dst_ref=scale_in.at[c, me],
                send_sem=s3_sem.at[c],
                recv_sem=r3_sem.at[c],
                device_id=(me_b, to),
                device_id_type=MESH,
            ).start()

        pltpu.make_async_copy(scale_out.at[c], scale_in.at[c, me], r3_sem.at[c]).start()

        @pl.loop(1, tiles)
        def _(i):
            to = lax.rem(me + i, tiles)
            pltpu.make_async_remote_copy(
                src_ref=send2.at[pl.ds(pl.multiple_of((c * tiles + to) * size, 8), size)],
                dst_ref=recv2.at[pl.ds(pl.multiple_of((c * tiles + me) * size, 8), size)],
                send_sem=s2_sem.at[c],
                recv_sem=r2_sem.at[c],
                device_id=(me_b, to),
                device_id_type=MESH,
            ).start()

        at = pl.ds(pl.multiple_of((c * tiles + me) * size, 8), size)
        pltpu.make_async_copy(send2.at[at], recv2.at[at], r2_sem.at[c]).start()

    def backward(c):
        at = pl.ds(pl.multiple_of(c * tiles * per * rows * 8, 32), tiles * per * rows * 8)
        pltpu.make_async_copy(recv2.at[at], recv2.at[at], r2_sem.at[c]).wait()
        pltpu.make_async_copy(scale_in.at[c], scale_in.at[c], r3_sem.at[c]).wait()

        @pl.loop(0, per)
        def _(k):
            pair = 2 * (c * per + k)

            def grains(t, half):
                return jnp.broadcast_to(scale_in[c, t, pl.ds(2 * k + half, 1)], (8, 128))

            for t in range(0, tiles, 2):
                at = slice(4 * t, 4 * t + 8)
                grain[0, at] = jnp.where(low_rows, grains(t, 0), grains(t + 1, 1))
                grain[1, at] = jnp.where(low_rows, grains(t + 1, 0), grains(t, 1))
            for r in range(rows):
                if r % 2 == 0:
                    both = []
                    for t in range(tiles):
                        row = ((c * tiles + t) * per + k) * rows * 8 + r * 8
                        both.append(recv2[pl.ds(pl.multiple_of(row, 16), 16)].astype(jnp.int32).astype(f32))
                pieces = [piece[8 * (r % 2) : 8 * (r % 2) + 8] for piece in both]
                waves = (
                    grain[0] * jnp.concatenate([jnp.where(low_rows, pieces[2 * t], pieces[2 * t + 1]) for t in range(16)], axis=0),
                    grain[1] * jnp.concatenate([jnp.where(low_rows, pieces[2 * t + 1], pieces[2 * t]) for t in range(16)], axis=0),
                )
                terms = []
                for s in range(2):
                    potential = times_right(times_left(left_ref[4 + s], waves[s]), right_ref[...])
                    terms.append(potential * held[r][index_ref[1, pair + s]].astype(f32))
                for j in range(tgt):
                    out_ref[j, r] += (
                        weight_ref[j, pair] * terms[0] + weight_ref[j, pair + 1] * terms[1]
                    )

    def keep(r):
        for i in range(own):
            held[r][i] = stage[i, r]

    for r in range(rows):
        event(r, 0)
        event(r, 1)
        if r == 0:
            for q in range(rows):
                keep(q)
            out_ref[...] = jnp.zeros_like(out_ref)
            scale_out[...] = jnp.zeros_like(scale_out)
            for e in range(2, 7):
                event(r, e)
        else:
            leftovers(r - 1)

            @pl.loop(0, 5)
            def _(step):
                for e in range(2, 7):
                    pl.when(step == e - 2)(functools.partial(event, r, e))
                pl.when(step < chunks)(functools.partial(forward, r - 1, step))

    leftovers(rows - 1)
    pl.loop(0, chunks)(functools.partial(forward, rows - 1))
    pl.loop(0, chunks)(turn)
    pl.loop(0, chunks)(backward)

    for way in range(2):
        for r in range(rows):
            ref = held[r].at[pl.ds(0, sum(caps))]
            pltpu.make_async_copy(ref, ref, ring_send.at[way, r]).wait()
    for c in range(chunks):
        for r in range(rows):
            ref = send1.at[r, pl.ds(0, (tiles - 1) * per * 8)]
            pltpu.make_async_copy(ref, ref, s1_sem.at[r, c]).wait()
        ref = send2.at[pl.ds(0, (tiles - 1) * per * rows * 8)]
        pltpu.make_async_copy(ref, ref, s2_sem.at[c]).wait()
        ref = scale_in.at[c, pl.ds(0, tiles - 1)]
        pltpu.make_async_copy(ref, ref, s3_sem.at[c]).wait()


def run_exchange(slots, chunks, caps, tiles, orbitals, index, order, weight, kern, left, right):
    own, rows, height, width = orbitals.shape
    tgt = weight.shape[0]
    per = slots // 2 // chunks
    total = chunks * tiles * per * 8
    room = regions(caps, own)[1]
    vmem = pl.BlockSpec(memory_space=pltpu.VMEM)
    smem = pl.BlockSpec(memory_space=pltpu.SMEM)
    groups = lax.axis_size("band")
    return pl.pallas_call(
        functools.partial(exchange_kernel, (groups, tiles, own, tgt, chunks, per, caps)),
        out_shape=jax.ShapeDtypeStruct((tgt, rows, height, width), f32),
        in_specs=[smem, smem, smem, pl.BlockSpec(memory_space=pl.ANY), vmem, vmem, vmem],
        out_specs=vmem,
        scratch_shapes=[pltpu.VMEM((room, height, width), bf16)] * rows
        + [
            pltpu.VMEM((own, rows, height, width), bf16),
            pltpu.VMEM((rows, total, width), f32),
            pltpu.VMEM((rows, total, width), f32),
            pltpu.VMEM((total * rows, width), jnp.int16),
            pltpu.VMEM((total * rows, width), jnp.int16),
            pltpu.VMEM((tiles * rows * 8, width), f32),
            pltpu.VMEM((2, height, width), f32),
            pltpu.VMEM((chunks, 8, width), f32),
            pltpu.VMEM((chunks, tiles, 8, width), f32),
            pltpu.SemaphoreType.DMA,
            pltpu.SemaphoreType.DMA((2, rows)),
            pltpu.SemaphoreType.DMA((2, rows, 7)),
            pltpu.SemaphoreType.DMA((rows, chunks)),
            pltpu.SemaphoreType.DMA((rows, chunks)),
            pltpu.SemaphoreType.DMA((chunks,)),
            pltpu.SemaphoreType.DMA((chunks,)),
            pltpu.SemaphoreType.DMA((chunks,)),
            pltpu.SemaphoreType.DMA((chunks,)),
        ],
        compiler_params=pltpu.CompilerParams(
            collective_id=slots, has_side_effects=True, vmem_limit_bytes=60 * 1024 * 1024
        ),
    )(index, order, weight, orbitals, left, right, kern)


def routes(partners, counts, groups, tgt, own):
    targets, part = partners.shape
    active = jnp.arange(part, dtype=jnp.int32)[None, :] < counts[:, None]
    home = jnp.arange(targets, dtype=jnp.int32)[:, None] // tgt
    hop = (home - partners // own + groups) % groups
    code = jnp.where(active, partners * groups + hop, -1).reshape(-1)
    every = jnp.arange(groups * own * groups, dtype=jnp.int32)
    need = jnp.any(code[:, None] == every[None, :], axis=0).reshape(groups, own, groups)
    up3 = jnp.where(need[:, :, 3], 3, jnp.where(need[:, :, 2], 2, need[:, :, 1].astype(jnp.int32)))
    down3 = jnp.where(need[:, :, 5], 3, jnp.where(need[:, :, 6], 2, need[:, :, 7].astype(jnp.int32)))
    opposite = need[:, :, 4]
    lane = jnp.arange(own, dtype=jnp.int32)

    def place(key):
        full = key * own + lane[None, :]
        return jnp.sum((full[:, None, :] < full[:, :, None]).astype(jnp.int32), axis=2)

    turn = place(jnp.where(opposite, down3 - up3, 100))
    halfway = (jnp.sum(opposite.astype(jnp.int32), axis=1, keepdims=True) + 1) // 2
    goes_up = opposite & (turn < halfway)
    far = jnp.stack([jnp.where(goes_up, 4, up3), jnp.where(opposite & ~goes_up, 4, down3)])
    ranks = jnp.stack([place(-far[0]), place(-far[1])])
    hops = jnp.arange(1, 5, dtype=jnp.int32)
    load = jnp.max(jnp.sum((far[..., None] >= hops).astype(jnp.int32), axis=2), axis=(0, 1))
    return ranks, goes_up, load


def pair_lists(partners, counts, ranks, goes_up, band_index, groups, tgt, own, slots):
    part = partners.shape[1]
    own_lists = lax.dynamic_slice_in_dim(partners, band_index * tgt, tgt, 0).reshape(-1)
    own_counts = lax.dynamic_slice_in_dim(counts, band_index * tgt, tgt, 0)
    slot = jnp.arange(part, dtype=jnp.int32)
    active = (slot[None, :] < own_counts[:, None]).reshape(-1)
    every = jnp.arange(tgt * part, dtype=jnp.int32)
    place = jnp.sum(((every[None, :] < every[:, None]) & active[None, :]).astype(jnp.int32), axis=1)
    chosen = active[None, :] & (place[None, :] == jnp.arange(slots, dtype=jnp.int32)[:, None])
    partner = jnp.sum(jnp.where(chosen, own_lists[None, :], 0), axis=1)
    which = jnp.sum(jnp.where(chosen, (every // part)[None, :], 0), axis=1)
    live = jnp.any(chosen, axis=1)
    weight = ((which[None, :] == jnp.arange(tgt)[:, None]) & live[None, :]).astype(f32)
    hop = (band_index - partner // own + groups) % groups
    band = partner[:, None] == jnp.arange(groups * own, dtype=jnp.int32)[None, :]
    rises = jnp.any(band & goes_up.reshape(1, -1), axis=1)
    way = ((hop > 4) | ((hop == 4) & ~rises)).astype(jnp.int32)
    rank = jnp.sum(jnp.where(band, jnp.where(way[:, None] > 0, ranks[1].reshape(1, -1), ranks[0].reshape(1, -1)), 0), axis=1)
    far = jnp.where(live, jnp.where(hop > 4, groups - hop, hop), 0)
    return which, partner % own, way, far, rank, weight


VARIANTS = (
    (16, 4, (7, 6, 5, 2)),
    (18, 3, (7, 6, 5, 2)),
    (20, 5, (8, 7, 6, 3)),
    (24, 4, (8, 8, 8, 4)),
)


def per_device(orbitals, partners, counts):
    own, depth, height, width = orbitals.shape
    groups = lax.axis_size("band")
    tiles = lax.axis_size("grid")
    total_depth = depth * tiles
    band_index = lax.axis_index("band")
    tgt = partners.shape[0] // groups
    slab_rows = height // tiles
    kernel = screened_kernel(
        frequency(total_depth, 0, total_depth),
        frequency(height, lax.axis_index("grid") * slab_rows, slab_rows),
        frequency(width, 0, width),
    )
    kernel = kernel / float(total_depth * height * width)
    left, right = tables(height, total_depth, tiles, depth)
    ranks, goes_up, load = routes(partners, counts, groups, tgt, own)
    most = jnp.max(jnp.sum(counts.reshape(groups, tgt), axis=1))
    slots = VARIANTS[-1][0]
    which, local, way, far, rank, weight = pair_lists(
        partners, counts, ranks, goes_up, band_index, groups, tgt, own, slots
    )
    own_ranks = lax.dynamic_slice_in_dim(ranks, band_index, 1, 1)[:, 0]
    lane = jnp.arange(own, dtype=jnp.int32)
    order = jnp.sum(jnp.where(own_ranks[:, None, :] == lane[None, :, None], lane[None, None, :], 0), axis=2)
    pick = jnp.int32(len(VARIANTS) - 1)
    for at in reversed(range(len(VARIANTS) - 1)):
        some, _, caps = VARIANTS[at]
        pick = jnp.where((most <= some) & jnp.all(load <= jnp.array(caps, jnp.int32)), at, pick)

    def branch(variant):
        some, chunks, caps = variant
        table, _ = regions(caps, own)

        def run(orbitals, which, local, way, far, rank, weight, order, kernel, left, right):
            slot = jnp.zeros_like(far)
            for w in range(2):
                for h in range(1, 5):
                    slot = jnp.where((way == w) & (far == h), table[w][h] + rank, slot)
            slot = jnp.where(far == 0, local, slot)
            index = jnp.stack([which, slot])[:, :some]
            return run_exchange(
                some, chunks, caps, tiles, orbitals, index, order, weight[:, :some], kernel, left, right
            )

        return run

    return lax.switch(
        pick,
        [branch(v) for v in VARIANTS],
        orbitals, which, local, way, far, rank, weight, order, kernel, jnp.asarray(left), jnp.asarray(right),
    )


def solution(mesh):
    return jax.shard_map(
        per_device,
        mesh=mesh,
        in_specs=(P("band", "grid", None, None), P(), P()),
        out_specs=P("band", "grid", None, None),
        check_vma=False,
    )
```

```python
import functools
import math

import jax
import jax.numpy as jnp
import ml_dtypes
import numpy as np
from jax import lax
from jax.experimental import pallas as pl
from jax.experimental.pallas import tpu as pltpu
from jax.sharding import PartitionSpec as P

screening = 0.032
MESH = pl.DeviceIdType.MESH
f32 = jnp.float32
bf16 = jnp.bfloat16


def frequency(length, start, count):
    index = start + jnp.arange(count, dtype=jnp.int32)
    folded = jnp.minimum(index, length - index).astype(f32)
    return 2.0 * math.pi / length * folded


def screened_kernel(z_freq, y_freq, x_freq):
    squared = z_freq[None, :, None] ** 2 + y_freq[:, None, None] ** 2 + x_freq[None, None, :] ** 2
    safe = jnp.where(squared > 0, squared, 1.0)
    values = 4.0 * math.pi * (1.0 - jnp.exp(-safe / (4.0 * screening * screening))) / safe
    return jnp.where(squared > 0, values, math.pi / (screening * screening))


def cas_table(length):
    index = np.arange(length)
    phase = (np.outer(index, index) % length) * (2.0 * np.pi / length)
    return np.cos(phase) + np.sin(phase)


def split_np(table):
    high = table.astype(ml_dtypes.bfloat16)
    low = (table - high.astype(np.float64)).astype(ml_dtypes.bfloat16)
    return high, low


def left_table(table):
    high, low = split_np(table)
    return np.concatenate([high, high, low], axis=1)


def tables(height, total, tiles, rows):
    cas = cas_table(height)
    swap = np.arange(height).reshape(-1, 2, rows)[:, ::-1].reshape(-1)
    cas_z = cas_table(total)
    order = np.arange(total)
    order = rows * (order % tiles) + order // tiles
    left = np.stack(
        [
            left_table(cas),
            left_table(cas[swap]),
            left_table(cas_z[:, order]),
            left_table(cas_z[order]),
            left_table(cas),
            left_table(cas[:, swap]),
        ]
    )
    high, low = split_np(cas)
    return left, np.concatenate([high, high, low], axis=0)


def split(value):
    high = value.astype(bf16)
    low = (value - high.astype(f32)).astype(bf16)
    return high, low


def times_right(value, table):
    high, low = split(value)
    return jnp.dot(jnp.concatenate([high, low, high], axis=1), table, preferred_element_type=f32)


def times_left(table, value):
    high, low = split(value)
    return jnp.dot(table, jnp.concatenate([high, low, high], axis=0), preferred_element_type=f32)


def regions(caps, own):
    first, table = own, []
    for _ in range(2):
        row = []
        for cap in (caps[0],) + tuple(caps):
            row.append(first)
            first += cap
        table.append(row)
    return table, first


def exchange_kernel(
    cfg,
    index_ref,
    order_ref,
    weight_ref,
    orb_ref,
    left_ref,
    right_ref,
    kern_ref,
    out_ref,
    held0,
    held1,
    held2,
    held3,
    stage,
    send1,
    recv1,
    send2,
    recv2,
    plain,
    grain,
    dense,
    other,
    scale_out,
    scale_in,
    own_sem,
    ring_send,
    ring_recv,
    s1_sem,
    r1_sem,
    s2_sem,
    r2_sem,
    s3_sem,
    r3_sem,
):
    groups, tiles, own, tgt, chunks, per, caps = cfg
    held = (held0, held1, held2, held3)
    rows = len(held)
    first, _ = regions(caps, own)
    me_b = lax.axis_index("band")
    me = lax.axis_index("grid")
    up = lax.rem(me_b + 1, groups)
    down = lax.rem(me_b + groups - 1, groups)

    fetch = pltpu.make_async_copy(orb_ref, stage, own_sem)
    fetch.start()
    barrier = pltpu.get_barrier_semaphore()
    for neighbour in (up, down):
        pl.semaphore_signal(barrier, inc=1, device_id=(neighbour, me), device_id_type=MESH)

    @pl.loop(1, tiles)
    def _(i):
        pl.semaphore_signal(
            barrier, inc=1, device_id=(me_b, lax.rem(me + i, tiles)), device_id_type=MESH
        )

    fetch.wait()
    for r in range(rows):
        for way in range(2):

            @pl.loop(0, caps[0])
            def _(s):
                held[r][first[way][0] + s] = stage[order_ref[way, s], r]

    pl.semaphore_wait(barrier, tiles + 1)

    def span(e):
        hop = e // 2
        cut = (caps[hop] + 1) // 2
        if e == 6:
            return hop, 0, caps[hop]
        return (hop, 0, cut) if e % 2 == 0 else (hop, cut, caps[hop])

    def event(r, e):
        hop, start, end = span(e)
        for way in range(2):
            if e >= 2:
                arrived(r, e - 2, way)
            pltpu.make_async_remote_copy(
                src_ref=held[r].at[pl.ds(first[way][hop] + start, end - start)],
                dst_ref=held[r].at[pl.ds(first[way][hop + 1] + start, end - start)],
                send_sem=ring_send.at[way, r],
                recv_sem=ring_recv.at[way, r, e],
                device_id=(down if way else up, me),
                device_id_type=MESH,
            ).start()

    def arrived(r, e, way):
        hop, start, end = span(e)
        ref = held[r].at[pl.ds(first[way][hop + 1] + start, end - start)]
        pltpu.make_async_copy(ref, ref, ring_recv.at[way, r, e]).wait()

    def leftovers(r):
        for way in range(2):
            arrived(r, 5, way)
            arrived(r, 6, way)

    low_rows = lax.broadcasted_iota(jnp.int32, (8, 128), 0) < 4

    def forward(r, c):
        @pl.loop(0, per)
        def _(k):
            pair = 2 * (c * per + k)
            for row in range(rows):

                @pl.when(r == row)
                def _():
                    for s in range(2):
                        target = held[row][index_ref[0, pair + s]].astype(f32)
                        dense[s] = target * held[row][index_ref[1, pair + s]].astype(f32)

            turned = []
            for s in range(2):
                along_x = times_right(dense[s], right_ref[...])
                turned.append(times_left(left_ref[s], along_x))
            one, two = turned
            for t in range(16):
                a, b = one[8 * t : 8 * t + 8], two[8 * t : 8 * t + 8]
                at = ((c * tiles + 2 * t) * per + k) * 8
                send1[r, pl.ds(pl.multiple_of(at, 8), 8)] = jnp.where(low_rows, a, b)
                at = ((c * tiles + 2 * t + 1) * per + k) * 8
                send1[r, pl.ds(pl.multiple_of(at, 8), 8)] = jnp.where(low_rows, b, a)

        size = per * 8

        @pl.loop(1, tiles)
        def _(i):
            to = lax.rem(me + i, tiles)
            pltpu.make_async_remote_copy(
                src_ref=send1.at[r, pl.ds(pl.multiple_of((c * tiles + to) * size, 8), size)],
                dst_ref=recv1.at[r, pl.ds(pl.multiple_of((c * tiles + me) * size, 8), size)],
                send_sem=s1_sem.at[r, c],
                recv_sem=r1_sem.at[r, c],
                device_id=(me_b, to),
                device_id_type=MESH,
            ).start()

        at = pl.ds(pl.multiple_of((c * tiles + me) * size, 8), size)
        pltpu.make_async_copy(send1.at[r, at], recv1.at[r, at], r1_sem.at[r, c]).start()

    size = rows * 8

    def turn(c):
        for r in range(rows):
            at = pl.ds(pl.multiple_of(c * tiles * per * 8, 8), tiles * per * 8)
            pltpu.make_async_copy(recv1.at[r, at], recv1.at[r, at], r1_sem.at[r, c]).wait()

        @pl.loop(0, per)
        def _(k):
            tops = []
            for q in range(0, 8, 2):
                columns = []
                for p in (q, q + 1):
                    columns.append(
                        jnp.concatenate(
                            [
                                recv1[r, pl.ds((c * tiles * per + k) * 8 + p, tiles, stride=per * 8)]
                                for r in range(rows)
                            ],
                            axis=0,
                        )
                    )
                image = times_left(left_ref[2], jnp.concatenate(columns, axis=1))
                image = image * jnp.concatenate([kern_ref[q % 4], kern_ref[q % 4 + 1]], axis=1)
                back = times_left(left_ref[3], image)
                for p in range(2):
                    part = back[:, p * 128 : (p + 1) * 128]
                    top = jnp.max(jnp.abs(part), axis=0, keepdims=True)
                    if (q + p) % 4 == 0:
                        tops.append(top)
                    else:
                        tops[-1] = jnp.maximum(tops[-1], top)
                    for r in range(rows):
                        plain[pl.ds(r * 8 + q + p, tiles, stride=rows * 8)] = part[r * tiles : (r + 1) * tiles]
            couple = c * per + k
            tops = [jnp.maximum(top, 1e-30) for top in tops]
            for p in range(2):
                scale_out[couple, pl.ds(p, 1)] = tops[p] * (1.0 / 32766.0)
            fine = jnp.where(
                low_rows,
                jnp.broadcast_to(32766.0 / tops[0], (8, 128)),
                jnp.broadcast_to(32766.0 / tops[1], (8, 128)),
            )
            fine = jnp.concatenate([fine] * rows, axis=0)
            for t in range(tiles):
                coded = jnp.round(plain[size * t : size * (t + 1)] * fine)
                send2[couple, pl.ds(t * size, size)] = coded.astype(jnp.int32).astype(jnp.int16)

            @pl.loop(1, tiles)
            def _(i):
                to = lax.rem(me + i, tiles)
                pltpu.make_async_remote_copy(
                    src_ref=scale_out.at[couple],
                    dst_ref=scale_in.at[couple, me],
                    send_sem=s3_sem.at[couple],
                    recv_sem=r3_sem.at[couple],
                    device_id=(me_b, to),
                    device_id_type=MESH,
                ).start()
                pltpu.make_async_remote_copy(
                    src_ref=send2.at[couple, pl.ds(pl.multiple_of(to * size, size), size)],
                    dst_ref=recv2.at[couple, pl.ds(pl.multiple_of(me * size, size), size)],
                    send_sem=s2_sem.at[couple],
                    recv_sem=r2_sem.at[couple],
                    device_id=(me_b, to),
                    device_id_type=MESH,
                ).start()

            at = pl.ds(pl.multiple_of(me * size, size), size)
            pltpu.make_async_copy(send2.at[couple, at], recv2.at[couple, at], r2_sem.at[couple]).start()
            pltpu.make_async_copy(scale_out.at[couple], scale_in.at[couple, me], r3_sem.at[couple]).start()

    def backward(couple):
        pltpu.make_async_copy(recv2.at[couple], recv2.at[couple], r2_sem.at[couple]).wait()
        pltpu.make_async_copy(scale_in.at[couple], scale_in.at[couple], r3_sem.at[couple]).wait()
        pair = 2 * couple
        coarse = [scale_in[couple, t] for t in range(tiles)]

        def grains(t, half):
            return jnp.broadcast_to(coarse[t][half : half + 1], (8, 128))

        for t in range(0, tiles, 2):
            at = slice(4 * t, 4 * t + 8)
            grain[0, at] = jnp.where(low_rows, grains(t, 0), grains(t + 1, 1))
            grain[1, at] = jnp.where(low_rows, grains(t + 1, 0), grains(t, 1))
        for r in range(rows):
            for s in range(2):
                other[r, s] = held[r][index_ref[1, pair + s]].astype(f32)

        @pl.loop(0, rows // 2)
        def _(two):
            both = []
            for t in range(tiles):
                at = pl.multiple_of(t * size + two * 16, 16)
                both.append(recv2[couple, pl.ds(at, 16)].astype(jnp.int32).astype(f32))
            for odd in range(2):
                r = 2 * two + odd
                pieces = [piece[8 * odd : 8 * odd + 8] for piece in both]
                waves = (
                    grain[0] * jnp.concatenate([jnp.where(low_rows, pieces[2 * t], pieces[2 * t + 1]) for t in range(16)], axis=0),
                    grain[1] * jnp.concatenate([jnp.where(low_rows, pieces[2 * t + 1], pieces[2 * t]) for t in range(16)], axis=0),
                )
                terms = []
                for s in range(2):
                    potential = times_right(times_left(left_ref[4 + s], waves[s]), right_ref[...])
                    terms.append(potential * other[r, s])
                for j in range(tgt):
                    out_ref[j, r] += (
                        weight_ref[j, pair] * terms[0] + weight_ref[j, pair + 1] * terms[1]
                    )

    event(0, 0)
    event(0, 1)

    @pl.loop(0, own)
    def _(i):
        for r in range(rows):
            held[r][i] = stage[i, r]

    @pl.loop(0, rows)
    def _(r):
        for j in range(tgt):
            out_ref[j, r] = jnp.zeros_like(out_ref[j, r])

    for e in range(2, 7):
        event(0, e)

    @pl.loop(1, rows + 1)
    def _(r):
        for row in range(1, rows):

            @pl.when(r == row)
            def _():
                event(row, 0)
                event(row, 1)

        for row in range(rows):
            pl.when(r == row + 1)(functools.partial(leftovers, row))

        @pl.loop(0, 5)
        def _(step):
            for row in range(1, rows):
                for e in range(2, 7):
                    pl.when((r == row) & (step == e - 2))(functools.partial(event, row, e))
            pl.when(step < chunks)(functools.partial(forward, r - 1, step))

    pl.loop(0, chunks)(turn)
    pl.loop(0, chunks * per)(backward)

    for way in range(2):
        for r in range(rows):
            ref = held[r].at[pl.ds(0, sum(caps))]
            pltpu.make_async_copy(ref, ref, ring_send.at[way, r]).wait()
    for c in range(chunks):
        for r in range(rows):
            ref = send1.at[r, pl.ds(0, (tiles - 1) * per * 8)]
            pltpu.make_async_copy(ref, ref, s1_sem.at[r, c]).wait()
    for couple in range(chunks * per):
        ref = send2.at[couple, pl.ds(0, (tiles - 1) * size)]
        pltpu.make_async_copy(ref, ref, s2_sem.at[couple]).wait()
        ref = scale_in.at[couple, pl.ds(0, tiles - 1)]
        pltpu.make_async_copy(ref, ref, s3_sem.at[couple]).wait()


def run_exchange(at, variant, tiles, orbitals, index, order, weight, kern, left, right):
    slots, chunks, caps = variant
    own, rows, height, width = orbitals.shape
    tgt = weight.shape[0]
    couples = slots // 2
    per = couples // chunks
    total = chunks * tiles * per * 8
    room = regions(caps, own)[1]
    vmem = pl.BlockSpec(memory_space=pltpu.VMEM)
    smem = pl.BlockSpec(memory_space=pltpu.SMEM)
    groups = lax.axis_size("band")
    return pl.pallas_call(
        functools.partial(exchange_kernel, (groups, tiles, own, tgt, chunks, per, caps)),
        out_shape=jax.ShapeDtypeStruct((tgt, rows, height, width), f32),
        in_specs=[smem, smem, smem, pl.BlockSpec(memory_space=pl.ANY), vmem, vmem, vmem],
        out_specs=vmem,
        scratch_shapes=[pltpu.VMEM((room, height, width), bf16)] * rows
        + [
            pltpu.VMEM((own, rows, height, width), bf16),
            pltpu.VMEM((rows, total, width), f32),
            pltpu.VMEM((rows, total, width), f32),
            pltpu.VMEM((couples, tiles * rows * 8, width), jnp.int16),
            pltpu.VMEM((couples, tiles * rows * 8, width), jnp.int16),
            pltpu.VMEM((tiles * rows * 8, width), f32),
            pltpu.VMEM((2, height, width), f32),
            pltpu.VMEM((2, height, width), f32),
            pltpu.VMEM((rows, 2, height, width), f32),
            pltpu.VMEM((couples, 2, width), f32),
            pltpu.VMEM((couples, tiles, 2, width), f32),
            pltpu.SemaphoreType.DMA,
            pltpu.SemaphoreType.DMA((2, rows)),
            pltpu.SemaphoreType.DMA((2, rows, 7)),
            pltpu.SemaphoreType.DMA((rows, chunks)),
            pltpu.SemaphoreType.DMA((rows, chunks)),
        ]
        + [pltpu.SemaphoreType.DMA((couples,))] * 4,
        compiler_params=pltpu.CompilerParams(
            collective_id=at + 1, has_side_effects=True, vmem_limit_bytes=60 * 1024 * 1024
        ),
    )(index, order, weight, orbitals, left, right, kern)


VARIANTS = (
    (18, 3, (6, 5, 4, 2)),
    (18, 3, (7, 6, 5, 2)),
    (20, 5, (8, 7, 6, 3)),
    (24, 4, (8, 8, 8, 4)),
)


def plan_kernel(
    cfg, partners_ref, counts_ref, pick_ref, index_ref, order_ref, weight_ref, info_ref, copy_ref, sem
):
    groups, own, tgt, part, slots = cfg
    me = lax.axis_index("band")
    lane = lax.broadcasted_iota(jnp.int32, (8, 128), 1)
    line = lax.broadcasted_iota(jnp.int32, (8, 128), 0)
    spot = lane % own

    def group_needs(g, carry):
        need, most = carry
        amount = jnp.int32(0)
        for j in range(tgt):
            count = counts_ref[g * tgt + j]
            for k in range(part):
                partner = partners_ref[g * tgt + j, k]
                hop = lax.rem(g - lax.div(partner, own) + groups, groups)
                active = count > k
                row = jnp.where(active, hop, 100)
                need = jnp.where((lane == partner) & (line == row), 1, need)
            amount = amount + count
        return need, jnp.maximum(most, amount)

    need, most = lax.fori_loop(
        0, groups, group_needs, (jnp.zeros((8, 128), jnp.int32), jnp.int32(0))
    )
    at_hop = [jnp.broadcast_to(need[h : h + 1], (8, 128)) for h in range(groups)]

    def peers(value):
        for j in range(1, own):
            yield jnp.where(spot + j < own, pltpu.roll(value, 128 - j, 1), pltpu.roll(value, own - j, 1))

    def place(key):
        full = key * own + spot
        rank = jnp.zeros((8, 128), jnp.int32)
        for other in peers(full):
            rank = rank + jnp.where(other < full, 1, 0)
        return rank

    def group_sum(value):
        total = value
        for other in peers(value):
            total = total + other
        return total

    def farthest(one, two, three):
        return jnp.where(three > 0, 3, jnp.where(two > 0, 2, one))

    up3 = farthest(at_hop[1], at_hop[2], at_hop[3])
    down3 = farthest(at_hop[7], at_hop[6], at_hop[5])
    opposite = at_hop[4]
    turn = place(jnp.where(opposite > 0, down3 - up3, 100))
    rises = jnp.where(turn < (group_sum(opposite) + 1) // 2, opposite, 0)
    far_up = jnp.where(rises > 0, 4, up3)
    far_down = jnp.where(opposite - rises > 0, 4, down3)
    info_ref[...] = place(-far_up) + 8 * place(-far_down) + 64 * rises
    copy = pltpu.make_async_copy(info_ref, copy_ref, sem)
    copy.start()
    load = [
        jnp.max(
            jnp.maximum(
                group_sum(jnp.where(far_up >= h, 1, 0)), group_sum(jnp.where(far_down >= h, 1, 0))
            )
        )
        for h in range(1, 5)
    ]
    pick = jnp.int32(len(VARIANTS) - 1)
    for at in reversed(range(len(VARIANTS) - 1)):
        some, _, caps = VARIANTS[at]
        fits = most <= some
        for h in range(4):
            fits = fits & (load[h] <= caps[h])
        pick = jnp.where(fits, at, pick)
    pick_ref[0] = pick

    def of_variant(values):
        chosen = jnp.int32(values[-1])
        for at in range(len(VARIANTS) - 1):
            chosen = jnp.where(pick == at, values[at], chosen)
        return chosen

    bases = [regions(variant[2], own)[0] for variant in VARIANTS]
    base = [[of_variant([table[w][h] for table in bases]) for h in range(5)] for w in range(2)]

    def clear(i, carry):
        for row in range(2):
            index_ref[row, i] = 0
        for j in range(tgt):
            weight_ref[j, i] = 0.0
        return carry

    lax.fori_loop(0, slots, clear, 0)
    copy.wait()
    for i in range(own):
        value = copy_ref[0, me * own + i]
        order_ref[0, lax.rem(value, 8)] = i
        order_ref[1, lax.rem(lax.div(value, 8), 8)] = i

    def one_target(j, slot):
        count = counts_ref[me * tgt + j]

        def one_pair(k, slot):
            partner = partners_ref[me * tgt + j, k]
            hop = lax.rem(me - lax.div(partner, own) + groups, groups)
            value = copy_ref[0, partner]
            falls = (hop > 4) | ((hop == 4) & (value < 64))
            rank = jnp.where(falls, lax.rem(lax.div(value, 8), 8), lax.rem(value, 8))
            distance = jnp.where(hop > 4, groups - hop, hop)
            first = jnp.int32(0)
            for h in range(1, 5):
                first = jnp.where(distance == h, jnp.where(falls, base[1][h], base[0][h]), first)
            index_ref[0, slot] = j
            index_ref[1, slot] = jnp.where(distance == 0, lax.rem(partner, own), first + rank)
            weight_ref[j, slot] = 1.0
            return slot + 1

        return lax.fori_loop(0, count, one_pair, slot)

    lax.fori_loop(0, tgt, one_target, jnp.int32(0))


def plan(partners, counts, groups, tgt, own):
    slots = max(variant[0] for variant in VARIANTS)
    smem = pl.BlockSpec(memory_space=pltpu.SMEM)
    return pl.pallas_call(
        functools.partial(plan_kernel, (groups, own, tgt, partners.shape[1], slots)),
        out_shape=[
            jax.ShapeDtypeStruct((1,), jnp.int32),
            jax.ShapeDtypeStruct((2, slots), jnp.int32),
            jax.ShapeDtypeStruct((2, own), jnp.int32),
            jax.ShapeDtypeStruct((tgt, slots), f32),
        ],
        in_specs=[smem, smem],
        out_specs=[smem] * 4,
        scratch_shapes=[
            pltpu.VMEM((8, 128), jnp.int32),
            pltpu.SMEM((8, 128), jnp.int32),
            pltpu.SemaphoreType.DMA,
        ],
    )(partners, counts)


def per_device(orbitals, partners, counts):
    own, depth, height, width = orbitals.shape
    groups = lax.axis_size("band")
    tiles = lax.axis_size("grid")
    total_depth = depth * tiles
    tgt = partners.shape[0] // groups
    slab_rows = height // tiles
    kernel = screened_kernel(
        frequency(total_depth, 0, total_depth),
        frequency(height, lax.axis_index("grid") * slab_rows, slab_rows),
        frequency(width, 0, width),
    )
    kernel = kernel / float(total_depth * height * width)
    left, right = tables(height, total_depth, tiles, depth)
    pick, index, order, weight = plan(partners, counts, groups, tgt, own)
    return lax.switch(
        pick[0],
        [functools.partial(run_exchange, at, variant, tiles) for at, variant in enumerate(VARIANTS)],
        orbitals, index, order, weight, kernel, jnp.asarray(left), jnp.asarray(right),
    )


def solution(mesh):
    return jax.shard_map(
        per_device,
        mesh=mesh,
        in_specs=(P("band", "grid", None, None), P(), P()),
        out_specs=P("band", "grid", None, None),
        check_vma=False,
    )
```

```python
import functools
import math

import jax
import jax.numpy as jnp
import ml_dtypes
import numpy as np
from jax import lax
from jax.experimental import pallas as pl
from jax.experimental.pallas import tpu as pltpu
from jax.sharding import PartitionSpec as P

screening = 0.032
MESH = pl.DeviceIdType.MESH
f32 = jnp.float32
bf16 = jnp.bfloat16


def squared_frequency(index, length):
    folded = jnp.minimum(index, length - index).astype(f32) * (2.0 * math.pi / length)
    return folded * folded


def screened_plane(y, height, shape):
    depth, width = shape
    z = lax.broadcasted_iota(jnp.int32, shape, 0)
    x = lax.broadcasted_iota(jnp.int32, shape, 1)
    squared = squared_frequency(z, depth) + squared_frequency(x, width)
    squared = squared + squared_frequency(jnp.full(shape, y, jnp.int32), height)
    safe = jnp.where(squared > 0, squared, 1.0)
    values = 4.0 * math.pi * (1.0 - jnp.exp(-safe / (4.0 * screening * screening))) / safe
    values = jnp.where(squared > 0, values, math.pi / (screening * screening))
    return values / float(depth * height * width)


def cas_table(length):
    index = np.arange(length)
    phase = (np.outer(index, index) % length) * (2.0 * np.pi / length)
    return np.cos(phase) + np.sin(phase)


def split_np(table):
    high = table.astype(ml_dtypes.bfloat16)
    low = (table - high.astype(np.float64)).astype(ml_dtypes.bfloat16)
    return high, low


def left_table(table):
    high, low = split_np(table)
    return np.concatenate([high, high, low], axis=1)


def tables(height, total, tiles, rows):
    cas = cas_table(height)
    swap = np.arange(height).reshape(-1, 2, rows)[:, ::-1].reshape(-1)
    cas_z = cas_table(total)
    order = np.arange(total)
    order = rows * (order % tiles) + order // tiles
    left = np.stack(
        [
            left_table(cas),
            left_table(cas[swap]),
            left_table(cas_z[:, order]),
            left_table(cas_z[order]),
            left_table(cas),
            left_table(cas[:, swap]),
        ]
    )
    high, low = split_np(cas)
    return left, np.concatenate([high, high, low], axis=0)


def split(value):
    high = value.astype(bf16)
    low = (value - high.astype(f32)).astype(bf16)
    return high, low


def times_right(value, table):
    high, low = split(value)
    return jnp.dot(jnp.concatenate([high, low, high], axis=1), table, preferred_element_type=f32)


def times_left(table, value):
    high, low = split(value)
    return jnp.dot(table, jnp.concatenate([high, low, high], axis=0), preferred_element_type=f32)


def regions(caps, own):
    first, table = own, []
    for _ in range(2):
        row = []
        for cap in (caps[0],) + tuple(caps):
            row.append(first)
            first += cap
        table.append(row)
    return table, first


def exchange_kernel(
    cfg,
    index_ref,
    order_ref,
    weight_ref,
    orb_ref,
    left_ref,
    right_ref,
    out_ref,
    held0,
    held1,
    held2,
    held3,
    stage,
    send1,
    recv1,
    send2,
    recv2,
    plain,
    grain,
    dense,
    other,
    scale_out,
    scale_in,
    tops_ref,
    kern_ref,
    own_sem,
    ring_send,
    ring_recv,
    s1_sem,
    r1_sem,
    s2_sem,
    r2_sem,
    s3_sem,
    r3_sem,
):
    groups, tiles, own, tgt, chunks, per, caps = cfg
    held = (held0, held1, held2, held3)
    rows = len(held)
    first, _ = regions(caps, own)
    me_b = lax.axis_index("band")
    me = lax.axis_index("grid")
    up = lax.rem(me_b + 1, groups)
    down = lax.rem(me_b + groups - 1, groups)

    fetch = pltpu.make_async_copy(orb_ref, stage, own_sem)
    fetch.start()
    barrier = pltpu.get_barrier_semaphore()
    for neighbour in (up, down):
        pl.semaphore_signal(barrier, inc=1, device_id=(neighbour, me), device_id_type=MESH)

    @pl.loop(1, tiles)
    def _(i):
        pl.semaphore_signal(
            barrier, inc=1, device_id=(me_b, lax.rem(me + i, tiles)), device_id_type=MESH
        )

    fetch.wait()
    for r in range(rows):
        for way in range(2):

            @pl.loop(0, caps[0])
            def _(s):
                held[r][first[way][0] + s] = stage[order_ref[way, s], r]

    pl.semaphore_wait(barrier, tiles + 1)

    def span(e):
        hop = e // 2
        cut = (caps[hop] + 1) // 2
        if e == 6:
            return hop, 0, caps[hop]
        return (hop, 0, cut) if e % 2 == 0 else (hop, cut, caps[hop])

    def event(r, e):
        hop, start, end = span(e)
        for way in range(2):
            if e >= 2:
                arrived(r, e - 2, way)
            pltpu.make_async_remote_copy(
                src_ref=held[r].at[pl.ds(first[way][hop] + start, end - start)],
                dst_ref=held[r].at[pl.ds(first[way][hop + 1] + start, end - start)],
                send_sem=ring_send.at[way, r],
                recv_sem=ring_recv.at[way, r, e],
                device_id=(down if way else up, me),
                device_id_type=MESH,
            ).start()

    def arrived(r, e, way):
        hop, start, end = span(e)
        ref = held[r].at[pl.ds(first[way][hop + 1] + start, end - start)]
        pltpu.make_async_copy(ref, ref, ring_recv.at[way, r, e]).wait()

    def leftovers(r):
        for way in range(2):
            arrived(r, 5, way)
            arrived(r, 6, way)

    low_rows = lax.broadcasted_iota(jnp.int32, (8, 128), 0) < 4

    def forward(r, c):
        @pl.loop(0, per)
        def _(k):
            pair = 2 * (c * per + k)
            for row in range(rows):

                @pl.when(r == row)
                def _():
                    for s in range(2):
                        target = held[row][index_ref[0, pair + s]].astype(f32)
                        dense[s] = target * held[row][index_ref[1, pair + s]].astype(f32)

            turned = []
            for s in range(2):
                along_x = times_right(dense[s], right_ref[...])
                turned.append(times_left(left_ref[s], along_x))
            one, two = turned
            for t in range(16):
                a, b = one[8 * t : 8 * t + 8], two[8 * t : 8 * t + 8]
                at = ((c * tiles + 2 * t) * per + k) * 8
                send1[r, pl.ds(pl.multiple_of(at, 8), 8)] = jnp.where(low_rows, a, b)
                at = ((c * tiles + 2 * t + 1) * per + k) * 8
                send1[r, pl.ds(pl.multiple_of(at, 8), 8)] = jnp.where(low_rows, b, a)

        size = per * 8

        @pl.loop(1, tiles)
        def _(i):
            to = lax.rem(me + i, tiles)
            pltpu.make_async_remote_copy(
                src_ref=send1.at[r, pl.ds(pl.multiple_of((c * tiles + to) * size, 8), size)],
                dst_ref=recv1.at[r, pl.ds(pl.multiple_of((c * tiles + me) * size, 8), size)],
                send_sem=s1_sem.at[r, c],
                recv_sem=r1_sem.at[r, c],
                device_id=(me_b, to),
                device_id_type=MESH,
            ).start()

        at = pl.ds(pl.multiple_of((c * tiles + me) * size, 8), size)
        pltpu.make_async_copy(send1.at[r, at], recv1.at[r, at], r1_sem.at[r, c]).start()

    size = rows * 8

    def turn(c):
        for r in range(rows):
            at = pl.ds(pl.multiple_of(c * tiles * per * 8, 8), tiles * per * 8)
            pltpu.make_async_copy(recv1.at[r, at], recv1.at[r, at], r1_sem.at[r, c]).wait()

        @pl.loop(0, per)
        def _(k):
            couple = c * per + k

            @pl.loop(0, 2)
            def _(half):
                for q in (0, 2):
                    columns = []
                    for p in (q, q + 1):
                        at = (c * tiles * per + k) * 8 + half * 4 + p
                        columns.append(
                            jnp.concatenate(
                                [recv1[r, pl.ds(at, tiles, stride=per * 8)] for r in range(rows)], axis=0
                            )
                        )
                    image = times_left(left_ref[2], jnp.concatenate(columns, axis=1))
                    image = image * jnp.concatenate([kern_ref[q], kern_ref[q + 1]], axis=1)
                    back = times_left(left_ref[3], image)
                    for p in range(2):
                        part = back[:, p * 128 : (p + 1) * 128]
                        for r in range(rows):
                            plain[pl.ds(r * 8 + half * 4 + q + p, tiles, stride=rows * 8)] = part[
                                r * tiles : (r + 1) * tiles
                            ]
                    top = jnp.max(jnp.abs(back), axis=0, keepdims=True)
                    top = jnp.maximum(top[:, :128], top[:, 128:])
                    if q == 0:
                        tops_ref[pl.ds(half, 1)] = jnp.maximum(top, 1e-30)
                    else:
                        tops_ref[pl.ds(half, 1)] = jnp.maximum(tops_ref[pl.ds(half, 1)], top)

            coarse = (tops_ref[0:2] * (1.00390625 / 32766.0)).astype(bf16)
            scale_out[couple] = coarse
            inverse = 1.0 / coarse.astype(f32)
            fine = jnp.where(
                low_rows,
                jnp.broadcast_to(inverse[0:1], (8, 128)),
                jnp.broadcast_to(inverse[1:2], (8, 128)),
            )
            fine = jnp.concatenate([fine] * rows, axis=0)
            for t in range(tiles):
                coded = jnp.round(plain[size * t : size * (t + 1)] * fine)
                send2[couple, pl.ds(t * size, size)] = coded.astype(jnp.int32).astype(jnp.int16)

            @pl.loop(1, tiles)
            def _(i):
                to = lax.rem(me + i, tiles)
                pltpu.make_async_remote_copy(
                    src_ref=scale_out.at[couple],
                    dst_ref=scale_in.at[couple, me],
                    send_sem=s3_sem.at[couple],
                    recv_sem=r3_sem.at[couple],
                    device_id=(me_b, to),
                    device_id_type=MESH,
                ).start()
                pltpu.make_async_remote_copy(
                    src_ref=send2.at[couple, pl.ds(pl.multiple_of(to * size, size), size)],
                    dst_ref=recv2.at[couple, pl.ds(pl.multiple_of(me * size, size), size)],
                    send_sem=s2_sem.at[couple],
                    recv_sem=r2_sem.at[couple],
                    device_id=(me_b, to),
                    device_id_type=MESH,
                ).start()

            at = pl.ds(pl.multiple_of(me * size, size), size)
            pltpu.make_async_copy(send2.at[couple, at], recv2.at[couple, at], r2_sem.at[couple]).start()
            pltpu.make_async_copy(scale_out.at[couple], scale_in.at[couple, me], r3_sem.at[couple]).start()

    def backward(couple):
        pltpu.make_async_copy(recv2.at[couple], recv2.at[couple], r2_sem.at[couple]).wait()
        pltpu.make_async_copy(scale_in.at[couple], scale_in.at[couple], r3_sem.at[couple]).wait()
        pair = 2 * couple
        coarse = [scale_in[couple, t].astype(f32) for t in range(tiles)]

        def grains(t, half):
            return jnp.broadcast_to(coarse[t][half : half + 1], (8, 128))

        for t in range(0, tiles, 2):
            at = slice(4 * t, 4 * t + 8)
            grain[0, at] = jnp.where(low_rows, grains(t, 0), grains(t + 1, 1))
            grain[1, at] = jnp.where(low_rows, grains(t + 1, 0), grains(t, 1))
        for r in range(rows):
            for s in range(2):
                other[r, s] = held[r][index_ref[1, pair + s]].astype(f32)

        @pl.loop(0, rows // 2)
        def _(two):
            both = []
            for t in range(tiles):
                at = pl.multiple_of(t * size + two * 16, 16)
                both.append(recv2[couple, pl.ds(at, 16)].astype(jnp.int32).astype(f32))
            for odd in range(2):
                r = 2 * two + odd
                pieces = [piece[8 * odd : 8 * odd + 8] for piece in both]
                waves = (
                    grain[0] * jnp.concatenate([jnp.where(low_rows, pieces[2 * t], pieces[2 * t + 1]) for t in range(16)], axis=0),
                    grain[1] * jnp.concatenate([jnp.where(low_rows, pieces[2 * t + 1], pieces[2 * t]) for t in range(16)], axis=0),
                )
                terms = []
                for s in range(2):
                    potential = times_right(times_left(left_ref[4 + s], waves[s]), right_ref[...])
                    terms.append(potential * other[r, s])
                for j in range(tgt):
                    out_ref[j, r] += (
                        weight_ref[j, pair] * terms[0] + weight_ref[j, pair + 1] * terms[1]
                    )

    event(0, 0)
    event(0, 1)

    @pl.loop(0, own)
    def _(i):
        for r in range(rows):
            held[r][i] = stage[i, r]

    @pl.loop(0, rows)
    def _(q):
        kern_ref[q] = screened_plane(me * rows + q, rows * tiles, kern_ref.shape[1:])

    @pl.loop(0, rows)
    def _(r):
        for j in range(tgt):
            out_ref[j, r] = jnp.zeros_like(out_ref[j, r])

    for e in range(2, 7):
        event(0, e)

    @pl.loop(1, rows + 1)
    def _(r):
        for row in range(1, rows):

            @pl.when(r == row)
            def _():
                event(row, 0)
                event(row, 1)

        for row in range(rows):
            pl.when(r == row + 1)(functools.partial(leftovers, row))

        @pl.loop(0, 5)
        def _(step):
            for row in range(1, rows):
                for e in range(2, 7):
                    pl.when((r == row) & (step == e - 2))(functools.partial(event, row, e))
            pl.when(step < chunks)(functools.partial(forward, r - 1, step))

    pl.loop(0, chunks)(turn)
    pl.loop(0, chunks * per)(backward)

    for way in range(2):
        for r in range(rows):
            ref = held[r].at[pl.ds(0, sum(caps))]
            pltpu.make_async_copy(ref, ref, ring_send.at[way, r]).wait()
    for c in range(chunks):
        for r in range(rows):
            ref = send1.at[r, pl.ds(0, (tiles - 1) * per * 8)]
            pltpu.make_async_copy(ref, ref, s1_sem.at[r, c]).wait()
    for couple in range(chunks * per):
        ref = send2.at[couple, pl.ds(0, (tiles - 1) * size)]
        pltpu.make_async_copy(ref, ref, s2_sem.at[couple]).wait()
        ref = scale_in.at[couple, pl.ds(0, tiles - 1)]
        pltpu.make_async_copy(ref, ref, s3_sem.at[couple]).wait()


def run_exchange(at, variant, tiles, orbitals, index, order, weight, left, right):
    slots, chunks, caps = variant
    own, rows, height, width = orbitals.shape
    tgt = weight.shape[0]
    couples = slots // 2
    per = couples // chunks
    total = chunks * tiles * per * 8
    room = regions(caps, own)[1]
    vmem = pl.BlockSpec(memory_space=pltpu.VMEM)
    smem = pl.BlockSpec(memory_space=pltpu.SMEM)
    groups = lax.axis_size("band")
    return pl.pallas_call(
        functools.partial(exchange_kernel, (groups, tiles, own, tgt, chunks, per, caps)),
        out_shape=jax.ShapeDtypeStruct((tgt, rows, height, width), f32),
        in_specs=[smem, smem, smem, pl.BlockSpec(memory_space=pl.ANY), vmem, vmem],
        out_specs=vmem,
        scratch_shapes=[pltpu.VMEM((room, height, width), bf16)] * rows
        + [
            pltpu.VMEM((own, rows, height, width), bf16),
            pltpu.VMEM((rows, total, width), f32),
            pltpu.VMEM((rows, total, width), f32),
            pltpu.VMEM((couples, tiles * rows * 8, width), jnp.int16),
            pltpu.VMEM((couples, tiles * rows * 8, width), jnp.int16),
            pltpu.VMEM((tiles * rows * 8, width), f32),
            pltpu.VMEM((2, height, width), f32),
            pltpu.VMEM((2, height, width), f32),
            pltpu.VMEM((rows, 2, height, width), f32),
            pltpu.VMEM((couples, 2, width), bf16),
            pltpu.VMEM((couples, tiles, 2, width), bf16),
            pltpu.VMEM((8, width), f32),
            pltpu.VMEM((rows, rows * tiles, width), f32),
            pltpu.SemaphoreType.DMA,
            pltpu.SemaphoreType.DMA((2, rows)),
            pltpu.SemaphoreType.DMA((2, rows, 7)),
            pltpu.SemaphoreType.DMA((rows, chunks)),
            pltpu.SemaphoreType.DMA((rows, chunks)),
        ]
        + [pltpu.SemaphoreType.DMA((couples,))] * 4,
        compiler_params=pltpu.CompilerParams(
            collective_id=at + 1, has_side_effects=True, vmem_limit_bytes=60 * 1024 * 1024
        ),
    )(index, order, weight, orbitals, left, right)


VARIANTS = (
    (18, 3, (6, 5, 4, 2)),
    (16, 4, (7, 6, 5, 2)),
    (18, 3, (7, 6, 5, 2)),
    (20, 5, (7, 6, 5, 2)),
    (20, 5, (8, 7, 6, 3)),
    (24, 4, (8, 8, 8, 4)),
)


def plan_kernel(
    cfg, partners_ref, counts_ref, pick_ref, index_ref, order_ref, weight_ref, info_ref, copy_ref, sem
):
    groups, own, tgt, part, slots = cfg
    me = lax.axis_index("band")
    lane = lax.broadcasted_iota(jnp.int32, (8, 128), 1)
    line = lax.broadcasted_iota(jnp.int32, (8, 128), 0)
    spot = lane % own

    def group_needs(g, carry):
        need, most = carry
        amount = jnp.int32(0)
        for j in range(tgt):
            count = counts_ref[g * tgt + j]
            for k in range(part):
                partner = partners_ref[g * tgt + j, k]
                hop = lax.rem(g - lax.div(partner, own) + groups, groups)
                active = count > k
                row = jnp.where(active, hop, 100)
                need = jnp.where((lane == partner) & (line == row), 1, need)
            amount = amount + count
        return need, jnp.maximum(most, amount)

    need, most = lax.fori_loop(
        0, groups, group_needs, (jnp.zeros((8, 128), jnp.int32), jnp.int32(0))
    )
    at_hop = [jnp.broadcast_to(need[h : h + 1], (8, 128)) for h in range(groups)]

    def peers(value):
        for j in range(1, own):
            yield jnp.where(spot + j < own, pltpu.roll(value, 128 - j, 1), pltpu.roll(value, own - j, 1))

    def place(key):
        full = key * own + spot
        rank = jnp.zeros((8, 128), jnp.int32)
        for other in peers(full):
            rank = rank + jnp.where(other < full, 1, 0)
        return rank

    def group_sum(value):
        total = value
        for other in peers(value):
            total = total + other
        return total

    def farthest(one, two, three):
        return jnp.where(three > 0, 3, jnp.where(two > 0, 2, one))

    up3 = farthest(at_hop[1], at_hop[2], at_hop[3])
    down3 = farthest(at_hop[7], at_hop[6], at_hop[5])
    opposite = at_hop[4]
    turn = place(jnp.where(opposite > 0, down3 - up3, 100))
    rises = jnp.where(turn < (group_sum(opposite) + 1) // 2, opposite, 0)
    far_up = jnp.where(rises > 0, 4, up3)
    far_down = jnp.where(opposite - rises > 0, 4, down3)
    info_ref[...] = place(-far_up) + 8 * place(-far_down) + 64 * rises
    copy = pltpu.make_async_copy(info_ref, copy_ref, sem)
    copy.start()
    load = [
        jnp.max(
            jnp.maximum(
                group_sum(jnp.where(far_up >= h, 1, 0)), group_sum(jnp.where(far_down >= h, 1, 0))
            )
        )
        for h in range(1, 5)
    ]
    pick = jnp.int32(len(VARIANTS) - 1)
    for at in reversed(range(len(VARIANTS) - 1)):
        some, _, caps = VARIANTS[at]
        fits = most <= some
        for h in range(4):
            fits = fits & (load[h] <= caps[h])
        pick = jnp.where(fits, at, pick)
    pick_ref[0] = pick

    def of_variant(values):
        chosen = jnp.int32(values[-1])
        for at in range(len(VARIANTS) - 1):
            chosen = jnp.where(pick == at, values[at], chosen)
        return chosen

    bases = [regions(variant[2], own)[0] for variant in VARIANTS]
    base = [[of_variant([table[w][h] for table in bases]) for h in range(5)] for w in range(2)]

    def clear(i, carry):
        for row in range(2):
            index_ref[row, i] = 0
        for j in range(tgt):
            weight_ref[j, i] = 0.0
        return carry

    lax.fori_loop(0, slots, clear, 0)
    copy.wait()
    for i in range(own):
        value = copy_ref[0, me * own + i]
        order_ref[0, lax.rem(value, 8)] = i
        order_ref[1, lax.rem(lax.div(value, 8), 8)] = i

    def one_target(j, slot):
        count = counts_ref[me * tgt + j]

        def one_pair(k, slot):
            partner = partners_ref[me * tgt + j, k]
            hop = lax.rem(me - lax.div(partner, own) + groups, groups)
            value = copy_ref[0, partner]
            falls = (hop > 4) | ((hop == 4) & (value < 64))
            rank = jnp.where(falls, lax.rem(lax.div(value, 8), 8), lax.rem(value, 8))
            distance = jnp.where(hop > 4, groups - hop, hop)
            first = jnp.int32(0)
            for h in range(1, 5):
                first = jnp.where(distance == h, jnp.where(falls, base[1][h], base[0][h]), first)
            index_ref[0, slot] = j
            index_ref[1, slot] = jnp.where(distance == 0, lax.rem(partner, own), first + rank)
            weight_ref[j, slot] = 1.0
            return slot + 1

        return lax.fori_loop(0, count, one_pair, slot)

    lax.fori_loop(0, tgt, one_target, jnp.int32(0))


def plan(partners, counts, groups, tgt, own):
    slots = max(variant[0] for variant in VARIANTS)
    smem = pl.BlockSpec(memory_space=pltpu.SMEM)
    return pl.pallas_call(
        functools.partial(plan_kernel, (groups, own, tgt, partners.shape[1], slots)),
        out_shape=[
            jax.ShapeDtypeStruct((1,), jnp.int32),
            jax.ShapeDtypeStruct((2, slots), jnp.int32),
            jax.ShapeDtypeStruct((2, own), jnp.int32),
            jax.ShapeDtypeStruct((tgt, slots), f32),
        ],
        in_specs=[smem, smem],
        out_specs=[smem] * 4,
        scratch_shapes=[
            pltpu.VMEM((8, 128), jnp.int32),
            pltpu.SMEM((8, 128), jnp.int32),
            pltpu.SemaphoreType.DMA,
        ],
    )(partners, counts)


def per_device(orbitals, partners, counts):
    own, depth, height, width = orbitals.shape
    groups = lax.axis_size("band")
    tiles = lax.axis_size("grid")
    total_depth = depth * tiles
    tgt = partners.shape[0] // groups
    left, right = tables(height, total_depth, tiles, depth)
    pick, index, order, weight = plan(partners, counts, groups, tgt, own)
    return lax.switch(
        pick[0],
        [functools.partial(run_exchange, at, variant, tiles) for at, variant in enumerate(VARIANTS)],
        orbitals, index, order, weight, jnp.asarray(left), jnp.asarray(right),
    )


def solution(mesh):
    return jax.shard_map(
        per_device,
        mesh=mesh,
        in_specs=(P("band", "grid", None, None), P(), P()),
        out_specs=P("band", "grid", None, None),
        check_vma=False,
    )
```
